32 devices in a mesh: grp: 1, head: 16 (over z, x, core), tile: 2 (over y).
Axes of the slice: x: 2, y: 2, z: 4, core: 2. Of those that a mesh axis runs over, the one named last changes fastest.
Arguments:
- attention: bfloat16 [144, 256, 256], P(('grp', 'head'), None, 'tile'), may hold values from 0 to 16, as said below
- proj_weight: bfloat16 [64, 144], replicated, may hold values from -0.5 to 0.5
- proj_bias: float32 [64], replicated, may hold values from -1.8 to 1.8
- conv_weight: bfloat16 [2, 2, 64, 64, 3, 3], replicated, may hold values from -0.25 to 0.25
- conv_bias: float32 [2, 2, 64], replicated, may hold values from -1.8 to 1.8
- out_weight: float32 [64], replicated, may hold values from -0.75 to 0.75
Outputs:
- logits: float32 [256, 256], P(('grp', 'head'), 'tile')
The draws below stay inside these ranges and needn't reach their ends.
Inputs may be any that keep to these rules, and one draw needn't show every extreme that they name: `attention`: every entry is positive.
All inputs are finite; a program needn't handle non-finite values.
Results may differ from the reference program's by a relative error of at most 0.007.
Values may be sent and summed in bfloat16 or wider, within the bound.
A program may use at most 128 MiB of HBM per device.

```python
import math
import jax
import jax.numpy as jnp
from jax import lax

MAPS = 144
FEAT = 64
BLOCKS = 2
W = 256


def draw_attention(key, part):
    keys = jax.random.split(jax.random.fold_in(key, 17), 4)
    row_scale = jnp.exp(jax.random.uniform(keys[0], (MAPS, W, 1), jnp.float32, 0.0, math.log(10.0)))
    col_scale = jnp.exp(jax.random.uniform(keys[1], (MAPS, 1, W), jnp.float32, 0.0, math.log(10.0)))
    entries = jax.random.uniform(keys[3], (MAPS, W, W), jnp.float32, 0.05, 1.0)
    return (row_scale * col_scale * entries / 16.0).astype(jnp.bfloat16)


def gaussian(key, extent, scale, most, dtype=jnp.bfloat16):
    return jnp.clip(scale * jax.random.normal(key, extent, jnp.float32), -most, most).astype(dtype)


def setup_inputs(seed: int = 0, part: int = 0) -> dict:
    streams_of = jax.random.split(jax.random.key(seed), 7)
    part_splits = jax.random.split(jax.random.fold_in(streams_of[6], part), 7)
    attention = draw_attention(jax.random.fold_in(jax.random.fold_in(streams_of[6], part), 71), part)
    proj_weight = gaussian(streams_of[1], (FEAT, MAPS), MAPS ** -0.5, 0.5)
    proj_bias = gaussian(streams_of[2], (FEAT,), 0.3, 1.8, jnp.float32)
    conv_weight = gaussian(streams_of[3], (BLOCKS, 2, FEAT, FEAT, 3, 3), (9 * FEAT) ** -0.5, 0.25)
    conv_bias = gaussian(streams_of[4], (BLOCKS, 2, FEAT), 0.3, 1.8, jnp.float32)
    out_weight = gaussian(streams_of[5], (FEAT,), FEAT ** -0.5, 0.75, jnp.float32)
    return dict(attention=attention, proj_weight=proj_weight, proj_bias=proj_bias, conv_weight=conv_weight, conv_bias=conv_bias, out_weight=out_weight)


def convolve(field, kernel, offsets):
    result = lax.conv_general_dilated(field[None], kernel.astype(jnp.float32), (1, 1), ((1, 1), (1, 1)), precision=lax.Precision.HIGHEST)[0]
    return result + offsets[:, None, None]


def reference(attention, proj_weight, proj_bias, conv_weight, conv_bias, out_weight):
    values = attention.astype(jnp.float32)
    symmetric = values + jnp.swapaxes(values, 1, 2)
    rowsum = jnp.sum(symmetric, axis=2)
    grand_total = jnp.sum(rowsum, axis=1)
    corrected = (symmetric - rowsum[:, :, None] * rowsum[:, None, :] / grand_total[:, None, None]).astype(jnp.bfloat16)
    stream = jnp.einsum('kc,crs->krs', proj_weight.astype(jnp.float32), corrected.astype(jnp.float32), precision=lax.Precision.HIGHEST)
    stream = (stream + proj_bias[:, None, None]).astype(jnp.bfloat16)
    for layer_index in range(BLOCKS):
        hidden = jax.nn.elu(convolve(stream.astype(jnp.float32), conv_weight[layer_index, 0], conv_bias[layer_index, 0])).astype(jnp.bfloat16)
        update = convolve(hidden.astype(jnp.float32), conv_weight[layer_index, 1], conv_bias[layer_index, 1])
        stream = (stream.astype(jnp.float32) + update).astype(jnp.bfloat16)
    return jnp.einsum('k,krs->rs', out_weight, stream.astype(jnp.float32), precision=lax.Precision.HIGHEST)
```

```python
import functools
import jax
import jax.numpy as jnp
from jax import lax
from jax.experimental import pallas as pl
from jax.experimental.pallas import tpu as pltpu
from jax.sharding import PartitionSpec as P

VM = pltpu.VMEM
BF = jnp.bfloat16
F32 = jnp.float32
MESH = pl.DeviceIdType.MESH


def remote(src, dst, send, recv, head, tile):
    return pltpu.make_async_remote_copy(
        src_ref=src,
        dst_ref=dst,
        send_sem=send,
        recv_sem=recv,
        device_id={"head": head, "tile": tile},
        device_id_type=MESH,
    )


def fold(head):
    pair, core = head // 2, lax.rem(head, 2)
    row, col = pair // 2, lax.rem(pair, 2)
    col = jnp.where(lax.rem(row, 2) == 0, col, 1 - col)
    return (row * 2 + col) * 2 + core


def spot_of(head, tile, nh):
    place = fold(head)
    return jnp.where(lax.rem(tile, 2) == 0, place, nh - 1 - place)


def head_of(spot, tile, nh):
    return fold(jnp.where(lax.rem(tile, 2) == 0, spot, nh - 1 - spot))


def kernel(
    nh, nt, a_hbm, pw_ref, pb_ref, cw_hbm, cb_ref, ow_ref, out_ref,
    a_ref, cw_ref, mirror, own, total, parts, corr, got, wide, weights, stream, stack, taps, logits,
    asem, wsem, msend, mrecv, psend, precv, gsend, grecv, lsem,
    hsend, hrecv, osend, orecv, ready,
):
    maps, width, cols = a_ref.shape
    band = got.shape[3]
    nd = nh * nt
    feat = pw_ref.shape[0]
    layers = cw_ref.shape[0]
    halo = 2 * layers
    rows = band + 2 * halo
    h = lax.axis_index("head")
    t = lax.axis_index("tile")
    here = spot_of(h, t, nh)
    spot = t * nh + here
    per = 3 if maps % 3 == 0 else maps
    chunks = maps // per

    load = pltpu.make_async_copy(a_hbm, a_ref, asem)
    load.start()
    load_weights = pltpu.make_async_copy(cw_hbm, cw_ref, wsem)
    load_weights.start()
    barrier = pltpu.get_barrier_semaphore()

    def greet(head, tile):
        pl.semaphore_signal(
            barrier, inc=1, device_id={"head": head, "tile": tile}, device_id_type=MESH
        )

    for k in range(1, nt):
        greet(h, lax.rem(t + k, nt))

    def greet_later(i, _):
        greet(i, t)
        return 0

    lax.fori_loop(h + 1, nh, greet_later, 0)
    pl.semaphore_wait(barrier, nt - 1 + h)

    def tell_earlier(i, _):
        pl.semaphore_signal(
            ready.at[h], inc=1, device_id={"head": h - 1 - i, "tile": t}, device_id_type=MESH
        )
        return 0

    def mirror_copy(k, q):
        p = lax.rem(t + k, nt)
        return remote(
            a_hbm.at[pl.ds(q * per, per), pl.ds(pl.multiple_of(p * cols, cols), cols), :],
            mirror.at[t, pl.ds(q * per, per)],
            msend.at[k - 1, q], mrecv.at[k - 1, q], h, p,
        )

    def parts_copy(k):
        p = lax.rem(t + k, nt)
        return remote(own, parts.at[k - 1], psend.at[k - 1], precv.at[k - 1], h, p)

    lax.fori_loop(0, h, tell_earlier, 0)

    load.wait()
    mine = pl.ds(pl.multiple_of(t * cols, cols), cols)
    ones_t = jnp.ones((8, cols), BF)
    ones_w = jnp.ones((8, width), BF)
    for c in range(maps):
        a = a_ref[c]
        line = lax.dot_general(ones_t, a, (((1,), (1,)), ((), ())), preferred_element_type=F32)
        own[c : c + 1, :] = line[0:1]
        columns = jnp.dot(ones_w, a, preferred_element_type=F32)
        own[c : c + 1, mine] = own[c : c + 1, mine] + columns[0:1]
    for k in range(1, nt):
        parts_copy(k).start()
    for k in range(1, nt):
        for q in range(chunks):
            mirror_copy(k, q).start()
    for k in range(1, nt):
        parts_copy(k).wait()
    sums = own[...]
    for k in range(1, nt):
        sums = sums + parts[k - 1]
    total[...] = sums
    grand = jnp.sum(sums, axis=1, keepdims=True)
    scaled = (total[:, mine] / grand).T

    for k in range(nt):
        p = lax.rem(t + k, nt)
        at = pl.ds(pl.multiple_of(p * cols, cols), cols)
        for q in range(chunks):
            if k:
                mirror_copy(k, q).wait()
            for c in range(q * per, (q + 1) * per):
                upright = a_ref[c, at, :].astype(F32).T
                across = (mirror[p, c] if k else a_ref[c, mine, :]).astype(F32)
                value = upright + (across - scaled[:, c : c + 1] * total[c : c + 1, at])
                corr[p, :, c] = value.astype(BF).reshape(nh, band, cols)

            def ship(i, _, k=k, q=q, p=p):
                head = lax.rem(h + i, nh)
                if k == 0 and q == 0:
                    @pl.when(head > h)
                    def _():
                        pl.semaphore_wait(ready.at[head], 1)
                remote(
                    corr.at[p, spot_of(head, t, nh), pl.ds(q * per, per)],
                    got.at[p, h, pl.ds(q * per, per)],
                    gsend.at[p], grecv.at[p], head, t,
                ).start()
                return 0

            lax.fori_loop(1, nh, ship, 0)
        pltpu.make_async_copy(corr.at[p, here], got.at[p, h], lsem.at[p]).start()

    def column(line):
        return jnp.broadcast_to(line, (8, feat)).T[:, 0:1]

    load_weights.wait()
    for layer in range(layers):
        for half in range(2):
            for dy in range(3):
                weights[layer, half, dy * feat : (dy + 1) * feat, :] = jnp.concatenate(
                    [cw_ref[layer, half, dy, dx].astype(F32) for dx in range(3)], axis=1
                ).astype(BF)
    proj_bias = column(pb_ref[...])

    def neighbour(step):
        band_there = lax.rem(spot + nd + step, nd)
        tile = band_there // nh
        return head_of(lax.rem(band_there, nh), tile, nh), tile

    up_head, up_tile = neighbour(-1)
    down_head, down_tile = neighbour(1)

    def halo_copies(p):
        at = pl.ds(pl.multiple_of(p * cols, cols), cols)
        to_up = remote(
            stream.at[pl.ds(halo, halo), :, at], stream.at[pl.ds(halo + band, halo), :, at],
            hsend.at[p, 0], hrecv.at[p, 0], up_head, up_tile,
        )
        to_down = remote(
            stream.at[pl.ds(band, halo), :, at], stream.at[pl.ds(0, halo), :, at],
            hsend.at[p, 1], hrecv.at[p, 1], down_head, down_tile,
        )
        return to_up, to_down

    for k in range(nt):
        p = lax.rem(t + k, nt)
        at = pl.ds(pl.multiple_of(p * cols, cols), cols)
        pltpu.make_async_copy(corr.at[p, here], got.at[p, h], lsem.at[p]).wait()
        rest = got.at[p, pl.ds(0, nh - 1)]
        pltpu.make_async_copy(rest, rest, grecv.at[p]).wait()
        wide[...] = got[p].astype(F32).reshape(nh * maps * band, cols)
        for r in range(band):
            x = wide[pl.ds(r, nh * maps, stride=band), :].astype(BF)
            value = jnp.dot(pw_ref[...], x, preferred_element_type=F32)
            stream[halo + r, :, at] = (value + proj_bias).astype(BF)
        for copy in halo_copies(p):
            copy.start()

    lane = lax.broadcasted_iota(jnp.int32, (feat, width), 1)
    first = spot * band - halo

    def put(r, v):
        if r < halo or r >= halo + band:
            g = first + r
            v = jnp.where(jnp.logical_and(g >= 0, g < nd * band), v, 0.0)
        before = jnp.where(lane == 0, 0.0, pltpu.roll(v, 1, 1))
        after = jnp.where(lane == width - 1, 0.0, pltpu.roll(v, width - 1, 1))
        stack[r, 0:feat] = before.astype(BF)
        stack[r, feat : 2 * feat] = v.astype(BF)
        stack[r, 2 * feat :] = after.astype(BF)

    def multiply(layer, half, r):
        taps[r] = jnp.dot(weights[layer, half], stack[r], preferred_element_type=F32)

    inner = range(halo, halo + band)
    outer = [r for r in range(rows) if r not in inner]
    readout = column(ow_ref[...])
    for layer in range(layers):
        for half in range(2):
            low = 2 * layer + half
            bias = column(cb_ref[layer, half : half + 1, :])
            if low == 0:
                for r in inner:
                    put(r, stream[r].astype(F32))
                    multiply(layer, half, r)
                for p in range(nt):
                    for copy in halo_copies(p):
                        copy.wait()
                for r in outer:
                    put(r, stream[r].astype(F32))
                    multiply(layer, half, r)
            else:
                for r in range(low, rows - low):
                    multiply(layer, half, r)
            for s in range(low + 1, rows - low - 1):
                conv = taps[s - 1, 0:feat] + taps[s, feat : 2 * feat] + taps[s + 1, 2 * feat :] + bias
                if half == 0:
                    put(s, jnp.where(conv > 0.0, conv, jnp.exp(jnp.minimum(conv, 0.0)) - 1.0))
                    continue
                value = (stream[s].astype(F32) + conv).astype(BF)
                if layer < layers - 1:
                    stream[s] = value
                    put(s, value.astype(F32))
                else:
                    line = jnp.sum(value.astype(F32) * readout, axis=0, keepdims=True)
                    for p in range(nt):
                        logits[p, s - halo : s - halo + 1, :] = line[:, p * cols : (p + 1) * cols]

    owner, slot = spot // nt, lax.rem(spot, nt)

    def deliver(k):
        p = lax.rem(t + k, nt)
        return remote(
            logits.at[p], out_ref.at[slot], osend.at[k], orecv.at[slot], owner, p,
        )

    for k in range(1, nt):
        deliver(k).start()

    @pl.when(owner == h)
    def _():
        pltpu.make_async_copy(logits.at[t], out_ref.at[slot], orecv.at[slot]).start()

    @pl.when(owner != h)
    def _():
        deliver(0).start()
        deliver(0).wait_send()

    for k in range(1, nt):
        deliver(k).wait_send()
    for p in range(nt):
        rest = got.at[p, pl.ds(0, nh - 1)]
        pltpu.make_async_copy(rest, rest, gsend.at[p]).wait()
    for k in range(nt):
        pltpu.make_async_copy(logits.at[k], out_ref.at[k], orecv.at[k]).wait()


def on_device(attention, proj_weight, proj_bias, conv_weight, conv_bias, out_weight):
    nh, nt = lax.axis_size("head"), lax.axis_size("tile")
    nd = nh * nt
    maps, width, cols = attention.shape
    layers, two, feat = conv_weight.shape[:3]
    band = width // nd
    far = max(nt - 1, 1)
    rows = band + 4 * layers
    ordered = jnp.transpose(conv_weight, (0, 1, 4, 5, 2, 3))
    dma = pltpu.SemaphoreType.DMA
    out = pl.pallas_call(
        functools.partial(kernel, nh, nt),
        out_shape=jax.ShapeDtypeStruct((nt, band, cols), F32),
        in_specs=[
            pl.BlockSpec(memory_space=pltpu.HBM),
            pl.BlockSpec(memory_space=VM),
            pl.BlockSpec(memory_space=VM),
            pl.BlockSpec(memory_space=pltpu.HBM),
            pl.BlockSpec(memory_space=VM),
            pl.BlockSpec(memory_space=VM),
        ],
        out_specs=pl.BlockSpec(memory_space=VM),
        scratch_shapes=[
            VM((maps, width, cols), BF),
            VM(ordered.shape, BF),
            VM((nt, maps, cols, cols), BF),
            VM((maps, width), F32),
            VM((maps, width), F32),
            VM((far, maps, width), F32),
            VM((nt, nh, maps, band, cols), BF),
            VM((nt, nh, maps, band, cols), BF),
            VM((nh * maps * band, cols), F32),
            VM((layers, two, 3 * feat, 3 * feat), BF),
            VM((rows, feat, width), BF),
            VM((rows, 3 * feat, width), BF),
            VM((rows, 3 * feat, width), F32),
            VM((nt, band, cols), F32),
            dma,
            dma,
            dma((far, maps)),
            dma((far, maps)),
            dma((far,)),
            dma((far,)),
            dma((nt,)),
            dma((nt,)),
            dma((nt,)),
            dma((nt, 2)),
            dma((nt, 2)),
            dma((nt,)),
            dma((nt,)),
            pltpu.SemaphoreType.REGULAR((nh,)),
        ],
        compiler_params=pltpu.CompilerParams(
            collective_id=0, has_side_effects=True, vmem_limit_bytes=56 * 1024 * 1024
        ),
        name="head",
    )(
        attention, proj_weight, proj_bias[None], ordered, conv_bias, out_weight[None],
    )
    return out.reshape(nt * band, cols)


def solution(mesh):
    return jax.shard_map(
        on_device,
        mesh=mesh,
        in_specs=(P(("grp", "head"), None, "tile"), P(), P(), P(), P(), P()),
        out_specs=P(("grp", "head"), "tile"),
        check_vma=False,
    )
```

```python
import functools
import jax
import jax.numpy as jnp
from jax import lax
from jax.experimental import pallas as pl
from jax.experimental.pallas import tpu as pltpu
from jax.sharding import PartitionSpec as P

VM = pltpu.VMEM
BF = jnp.bfloat16
F32 = jnp.float32
MESH = pl.DeviceIdType.MESH


def remote(src, dst, send, recv, head, tile):
    return pltpu.make_async_remote_copy(
        src_ref=src,
        dst_ref=dst,
        send_sem=send,
        recv_sem=recv,
        device_id={"head": head, "tile": tile},
        device_id_type=MESH,
    )


def fold(head):
    pair, core = head // 2, lax.rem(head, 2)
    row, col = pair // 2, lax.rem(pair, 2)
    col = jnp.where(lax.rem(row, 2) == 0, col, 1 - col)
    return (row * 2 + col) * 2 + core


def spot_of(head, tile, nh):
    place = fold(head)
    return jnp.where(lax.rem(tile, 2) == 0, place, nh - 1 - place)


def head_of(spot, tile, nh):
    return fold(jnp.where(lax.rem(tile, 2) == 0, spot, nh - 1 - spot))


def kernel(
    nh, nt, a_hbm, pw_hbm, pb_hbm, cw_hbm, cb_hbm, ow_hbm, out_ref,
    a_ref, pw_ref, pb_ref, cw_ref, cb_ref, ow_ref, mirror, both, own, total, parts, corr, got, wide, weights, stream, fresh, stack, taps, logits,
    asem, wsem, msend, mrecv, psend, precv, gsend, grecv, lsem,
    hsend, hrecv, osend, orecv, ready,
):
    maps, width, cols = a_ref.shape
    band = got.shape[3]
    nd = nh * nt
    feat = pw_ref.shape[0]
    layers = cw_ref.shape[0]
    halo = 2 * layers
    rows = band + 2 * halo
    h = lax.axis_index("head")
    t = lax.axis_index("tile")
    here = spot_of(h, t, nh)
    spot = t * nh + here
    per = 3 if maps % 3 == 0 else maps
    chunks = maps // per

    load = pltpu.make_async_copy(a_hbm, a_ref, asem)
    load.start()
    barrier = pltpu.get_barrier_semaphore()

    def greet(head, tile):
        pl.semaphore_signal(
            barrier, inc=1, device_id={"head": head, "tile": tile}, device_id_type=MESH
        )

    for k in range(1, nt):
        greet(h, lax.rem(t + k, nt))

    def greet_later(i, _):
        greet(i, t)
        return 0

    lax.fori_loop(h + 1, nh, greet_later, 0)
    load_weights = [
        pltpu.make_async_copy(src, dst, wsem.at[i])
        for i, (src, dst) in enumerate((
            (cw_hbm, cw_ref), (pw_hbm, pw_ref), (pb_hbm, pb_ref), (cb_hbm, cb_ref), (ow_hbm, ow_ref)
        ))
    ]
    for copy in load_weights:
        copy.start()
    pl.semaphore_wait(barrier, nt - 1 + h)

    def tell_earlier(i, _):
        pl.semaphore_signal(
            ready.at[h], inc=1, device_id={"head": i, "tile": t}, device_id_type=MESH
        )
        return 0

    def mirror_copy(k, q):
        p = lax.rem(t + k, nt)
        return remote(
            a_hbm.at[pl.ds(q * per, per), pl.ds(pl.multiple_of(p * cols, cols), cols), :],
            mirror.at[t, pl.ds(q * per, per)],
            msend.at[k - 1, q], mrecv.at[k - 1, q], h, p,
        )

    def parts_copy(k):
        p = lax.rem(t + k, nt)
        return remote(own, parts.at[k - 1], psend.at[k - 1], precv.at[k - 1], h, p)

    lax.fori_loop(0, h, tell_earlier, 0)

    load.wait()
    mine = pl.ds(pl.multiple_of(t * cols, cols), cols)
    ones_t = jnp.ones((8, cols), BF)
    ones_w = jnp.ones((8, width), BF)
    for c in range(maps):
        a = a_ref[c]
        line = lax.dot_general(ones_t, a, (((1,), (1,)), ((), ())), preferred_element_type=F32)
        own[c : c + 1, :] = line[0:1]
        columns = jnp.dot(ones_w, a, preferred_element_type=F32)
        own[c : c + 1, mine] = own[c : c + 1, mine] + columns[0:1]
    for k in range(1, nt):
        parts_copy(k).start()
    for k in range(1, nt):
        for q in range(chunks):
            mirror_copy(k, q).start()
    for c in range(maps):
        a = a_ref[c, mine, :].astype(F32)
        both[c] = a + a.T
    for k in range(1, nt):
        parts_copy(k).wait_recv()
    sums = own[...]
    for k in range(1, nt):
        sums = sums + parts[k - 1]
    total[...] = sums
    grand = jnp.sum(sums, axis=1, keepdims=True)
    scaled = (total[:, mine] / grand).T

    plane = 4 if nh % 8 == 0 else nh
    planes = nh // plane
    away = jnp.where(h < nh // 2, planes // 2, 0)

    def ship(p, low, count, wait=False):
        def step(i, _):
            head = lax.rem(i // plane + away, planes) * plane + lax.rem(i + h, plane)

            @pl.when(head != h)
            def _():
                if wait:
                    @pl.when(head > h)
                    def _():
                        pl.semaphore_wait(ready.at[head], 1)
                remote(
                    corr.at[p, spot_of(head, t, nh), pl.ds(low, count)],
                    got.at[p, h, pl.ds(low, count)],
                    gsend.at[p], grecv.at[p], head, t,
                ).start()
            return 0

        lax.fori_loop(0, nh, step, 0)

    for c in range(maps):
        value = both[c] - scaled[:, c : c + 1] * total[c : c + 1, mine]
        corr[t, :, c] = value.astype(BF).reshape(nh, band, cols)
    ship(t, 0, maps, True)
    for k in range(1, nt):
        p = lax.rem(t + k, nt)
        at = pl.ds(pl.multiple_of(p * cols, cols), cols)
        for q in range(chunks):
            mirror_copy(k, q).wait_recv()
            for c in range(q * per, (q + 1) * per):
                upright = a_ref[c, at, :].astype(F32).T
                across = mirror[p, c].astype(F32)
                value = upright + (across - scaled[:, c : c + 1] * total[c : c + 1, at])
                corr[p, :, c] = value.astype(BF).reshape(nh, band, cols)
            ship(p, q * per, per)
    for p in range(nt):
        pltpu.make_async_copy(corr.at[p, here], got.at[p, h], lsem.at[p]).start()

    def column(line):
        return jnp.broadcast_to(line, (8, feat)).T[:, 0:1]

    for copy in load_weights:
        copy.wait()
    for layer in range(layers):
        for half in range(2):
            for dy in range(3):
                weights[layer, half, dy * feat : (dy + 1) * feat, :] = jnp.concatenate(
                    [cw_ref[layer, half, dy, dx].astype(F32) for dx in range(3)], axis=1
                ).astype(BF)
    proj_bias = column(pb_ref[...])

    def neighbour(step):
        band_there = lax.rem(spot + nd + step, nd)
        tile = band_there // nh
        return head_of(lax.rem(band_there, nh), tile, nh), tile

    up_head, up_tile = neighbour(-1)
    down_head, down_tile = neighbour(1)

    def halo_copies(p):
        to_up = remote(
            stream.at[p, pl.ds(halo, halo)], stream.at[p, pl.ds(halo + band, halo)],
            hsend.at[p, 0], hrecv.at[p, 0], up_head, up_tile,
        )
        to_down = remote(
            stream.at[p, pl.ds(band, halo)], stream.at[p, pl.ds(0, halo)],
            hsend.at[p, 1], hrecv.at[p, 1], down_head, down_tile,
        )
        return to_up, to_down

    for k in range(nt):
        p = lax.rem(t + k, nt)
        pltpu.make_async_copy(corr.at[p, here], got.at[p, h], lsem.at[p]).wait()
        rest = got.at[p, pl.ds(0, nh - 1)]
        pltpu.make_async_copy(rest, rest, grecv.at[p]).wait()
        wide[...] = got[p].astype(F32).reshape(nh * maps * band, cols)
        to_up, to_down = halo_copies(p)
        for r in range(band):
            x = wide[pl.ds(r, nh * maps, stride=band), :].astype(BF)
            value = jnp.dot(pw_ref[...], x, preferred_element_type=F32)
            stream[p, halo + r] = (value + proj_bias).astype(BF)
            if r == halo - 1:
                to_up.start()
        to_down.start()

    lane = lax.broadcasted_iota(jnp.int32, (feat, width), 1)
    first = spot * band - halo

    def put(r, v):
        if r < halo or r >= halo + band:
            g = first + r
            v = jnp.where(jnp.logical_and(g >= 0, g < nd * band), v, 0.0)
        before = jnp.where(lane == 0, 0.0, pltpu.roll(v, 1, 1))
        after = jnp.where(lane == width - 1, 0.0, pltpu.roll(v, width - 1, 1))
        stack[r, 0:feat] = before.astype(BF)
        stack[r, feat : 2 * feat] = v.astype(BF)
        stack[r, 2 * feat :] = after.astype(BF)

    def line_of(r, kept=stream):
        return jnp.concatenate([kept[p, r] for p in range(nt)], axis=1).astype(F32)

    readout = column(ow_ref[...])
    biases = [column(cb_ref[low // 2, low % 2 : low % 2 + 1, :]) for low in range(2 * layers)]
    last = 2 * layers - 1

    def multiply(low, r):
        if low == 0:
            put(r, line_of(r))
        taps[low % 2, r] = jnp.dot(
            weights[low // 2, low % 2], stack[r], preferred_element_type=F32
        )

    def gather(low, s):
        part = taps.at[low % 2]
        conv = part[s - 1, 0:feat] + part[s, feat : 2 * feat] + part[s + 1, 2 * feat :] + biases[low]
        if low % 2 == 0:
            put(s, jnp.where(conv > 0.0, conv, jnp.exp(jnp.minimum(conv, 0.0)) - 1.0))
            return
        value = (line_of(s, stream if low == 1 else fresh) + conv).astype(BF)
        if low < last:
            for p in range(nt):
                fresh[p, s] = value[:, p * cols : (p + 1) * cols]
            put(s, value.astype(F32))
            return
        line = jnp.sum(value.astype(F32) * readout, axis=0, keepdims=True)
        for p in range(nt):
            logits[p, s - halo : s - halo + 1, :] = line[:, p * cols : (p + 1) * cols]

    early = {}
    for low in range(2 * layers):
        early[low] = range(halo + low, halo + band - low)
        for r in early[low]:
            multiply(low, r)
        for s in early[low][1:-1]:
            gather(low, s)
    for p in range(nt):
        for copy in halo_copies(p):
            copy.wait_recv()
    for low in range(2 * layers):
        for r in range(low, rows - low):
            if r not in early[low]:
                multiply(low, r)
        for s in range(low + 1, rows - low - 1):
            if s not in early[low][1:-1]:
                gather(low, s)

    owner, slot = spot // nt, lax.rem(spot, nt)

    def deliver(k):
        p = lax.rem(t + k, nt)
        return remote(
            logits.at[p], out_ref.at[slot], osend.at[k], orecv.at[slot], owner, p,
        )

    for k in range(1, nt):
        deliver(k).start()

    @pl.when(owner == h)
    def _():
        pltpu.make_async_copy(logits.at[t], out_ref.at[slot], orecv.at[slot]).start()

    @pl.when(owner != h)
    def _():
        deliver(0).start()
        deliver(0).wait_send()

    for k in range(1, nt):
        deliver(k).wait_send()
        parts_copy(k).wait_send()
        for q in range(chunks):
            mirror_copy(k, q).wait_send()
    for p in range(nt):
        for copy in halo_copies(p):
            copy.wait_send()
    for p in range(nt):
        rest = got.at[p, pl.ds(0, nh - 1)]
        pltpu.make_async_copy(rest, rest, gsend.at[p]).wait()
    for k in range(nt):
        pltpu.make_async_copy(logits.at[k], out_ref.at[k], orecv.at[k]).wait()


def on_device(attention, proj_weight, proj_bias, conv_weight, conv_bias, out_weight):
    nh, nt = lax.axis_size("head"), lax.axis_size("tile")
    nd = nh * nt
    maps, width, cols = attention.shape
    layers, two, feat = conv_weight.shape[:3]
    band = width // nd
    far = max(nt - 1, 1)
    rows = band + 4 * layers
    ordered = jnp.transpose(conv_weight, (0, 1, 4, 5, 2, 3))
    dma = pltpu.SemaphoreType.DMA
    out = pl.pallas_call(
        functools.partial(kernel, nh, nt),
        out_shape=jax.ShapeDtypeStruct((nt, band, cols), F32),
        in_specs=[pl.BlockSpec(memory_space=pltpu.HBM)] * 6,
        out_specs=pl.BlockSpec(memory_space=pl.ANY),
        scratch_shapes=[
            VM((maps, width, cols), BF),
            VM(proj_weight.shape, BF),
            VM((1, feat), F32),
            VM(ordered.shape, BF),
            VM(conv_bias.shape, F32),
            VM((1, feat), F32),
            VM((nt, maps, cols, cols), BF),
            VM((maps, cols, cols), F32),
            VM((maps, width), F32),
            VM((maps, width), F32),
            VM((far, maps, width), F32),
            VM((nt, nh, maps, band, cols), BF),
            VM((nt, nh, maps, band, cols), BF),
            VM((nh * maps * band, cols), F32),
            VM((layers, two, 3 * feat, 3 * feat), BF),
            VM((nt, rows, feat, cols), BF),
            VM((nt, rows, feat, cols), BF),
            VM((rows, 3 * feat, width), BF),
            VM((2, rows, 3 * feat, width), F32),
            VM((nt, band, cols), F32),
            dma,
            dma((5,)),
            dma((far, maps)),
            dma((far, maps)),
            dma((far,)),
            dma((far,)),
            dma((nt,)),
            dma((nt,)),
            dma((nt,)),
            dma((nt, 2)),
            dma((nt, 2)),
            dma((nt,)),
            dma((nt,)),
            pltpu.SemaphoreType.REGULAR((nh,)),
        ],
        compiler_params=pltpu.CompilerParams(
            collective_id=0, has_side_effects=True, vmem_limit_bytes=56 * 1024 * 1024
        ),
        name="head",
    )(
        attention, proj_weight, proj_bias[None], ordered, conv_bias, out_weight[None],
    )
    return out.reshape(nt * band, cols)


def solution(mesh):
    return jax.shard_map(
        on_device,
        mesh=mesh,
        in_specs=(P(("grp", "head"), None, "tile"), P(), P(), P(), P(), P()),
        out_specs=P(("grp", "head"), "tile"),
        check_vma=False,
    )
```

```python
import functools
import jax
import jax.numpy as jnp
import numpy as np
from jax import lax
from jax.experimental import pallas as pl
from jax.experimental.pallas import tpu as pltpu
from jax.sharding import PartitionSpec as P

VM = pltpu.VMEM
BF = jnp.bfloat16
F32 = jnp.float32
MESH = pl.DeviceIdType.MESH


def remote(src, dst, send, recv, head, tile):
    return pltpu.make_async_remote_copy(
        src_ref=src,
        dst_ref=dst,
        send_sem=send,
        recv_sem=recv,
        device_id={"head": head, "tile": tile},
        device_id_type=MESH,
    )


def fold(head):
    pair, core = head // 2, lax.rem(head, 2)
    row, col = pair // 2, lax.rem(pair, 2)
    col = jnp.where(lax.rem(row, 2) == 0, col, 1 - col)
    return (row * 2 + col) * 2 + core


def spot_of(head, tile, nh):
    place = fold(head)
    return jnp.where(lax.rem(tile, 2) == 0, place, nh - 1 - place)


def head_of(spot, tile, nh):
    return fold(jnp.where(lax.rem(tile, 2) == 0, spot, nh - 1 - spot))


def kernel(
    nh, nt, a_hbm, pw_hbm, pb_hbm, cw_hbm, cb_hbm, ow_hbm, tgt_hbm, out_ref,
    a_ref, pw_ref, pb_ref, cw_ref, cb_ref, ow_ref, tgt_ref, mirror, both, upright, scaled, own, total, parts, corr, got, wide, pwide, weights,
    sm, se, um, ue, stack, stack_e, taps, taps_e, logits, rows_w, rows_t, turned,
    asem, wsem, msend, mrecv, psend, precv, gsend, grecv, lsem,
    hsend, hrecv, osend, orecv, tsend, trecv, ready,
):
    maps, width, cols = a_ref.shape
    slots, band = got.shape[1:3]
    nd = nh * nt
    half_w = width // 2
    mains = half_w // cols
    feat = pw_ref.shape[0]
    layers = cw_ref.shape[0]
    halo = 2 * layers
    rows = band + 2 * halo
    edge = 3 * band + 2 * halo
    pack = cols // edge
    start = half_w - 2 * halo
    h = lax.axis_index("head")
    t = lax.axis_index("tile")
    here = spot_of(h, t, nh)
    spot = t * nh + here

    def slot_of(c, m=0):
        return c * mains + m + c // pack

    load = pltpu.make_async_copy(a_hbm, a_ref, asem)
    load.start()
    barrier = pltpu.get_barrier_semaphore()

    def greet(head, tile):
        pl.semaphore_signal(
            barrier, inc=1, device_id={"head": head, "tile": tile}, device_id_type=MESH
        )

    for k in range(1, nt):
        greet(h, lax.rem(t + k, nt))

    def greet_later(i, _):
        greet(i, t)
        return 0

    lax.fori_loop(h + 1, nh, greet_later, 0)
    load_weights = [
        pltpu.make_async_copy(src, dst, wsem.at[i])
        for i, (src, dst) in enumerate((
            (cw_hbm, cw_ref), (pw_hbm, pw_ref), (pb_hbm, pb_ref), (cb_hbm, cb_ref), (ow_hbm, ow_ref),
            (tgt_hbm, tgt_ref),
        ))
    ]
    for copy in load_weights:
        copy.start()
    pl.semaphore_wait(barrier, nt - 1 + h)

    def tell_earlier(i, _):
        pl.semaphore_signal(
            ready.at[h], inc=1, device_id={"head": i, "tile": t}, device_id_type=MESH
        )
        return 0

    lots = nh // 2
    step_rows = 2 * band

    def lot_of(j, tile):
        other = (h < nh // 2) == (lax.rem(tile, 2) == 0)
        return lax.rem(j + jnp.where(other, lots // 2, 0), lots)

    def mirror_copy(k, j, to):
        p = lax.rem(t + k, nt)
        low = pl.multiple_of(lot_of(j, p if to else t) * step_rows, step_rows)
        return remote(
            a_hbm.at[:, pl.ds(pl.multiple_of(p * cols + low, step_rows), step_rows), :],
            mirror.at[t, :, pl.ds(low, step_rows)],
            msend.at[k - 1, j], mrecv.at[k - 1, j], h, p,
        )

    def parts_copy(k):
        p = lax.rem(t + k, nt)
        return remote(own, parts.at[k - 1], psend.at[k - 1], precv.at[k - 1], h, p)

    for k in range(1, nt):
        mirror_copy(k, 0, True).start()
    lax.fori_loop(0, h, tell_earlier, 0)

    load.wait()
    mine = pl.ds(pl.multiple_of(t * cols, cols), cols)
    ones_t = jnp.ones((8, cols), BF)
    ones_w = jnp.ones((8, width), BF)
    for c in range(maps):
        a = a_ref[c]
        line = lax.dot_general(ones_t, a, (((1,), (1,)), ((), ())), preferred_element_type=F32)
        own[c : c + 1, :] = line[0:1]
        columns = jnp.dot(ones_w, a, preferred_element_type=F32)
        own[c : c + 1, mine] = own[c : c + 1, mine] + columns[0:1]
    for k in range(1, nt):
        parts_copy(k).start()
    for k in range(1, nt):
        for j in range(1, lots):
            mirror_copy(k, j, True).start()
    for c in range(maps):
        a = a_ref[c, mine, :].astype(F32)
        both[c] = a + a.T
        for k in range(1, nt):
            at = pl.ds(pl.multiple_of(lax.rem(t + k, nt) * cols, cols), cols)
            upright[k - 1, c] = a_ref[c, at, :].astype(F32).T
    for k in range(1, nt):
        parts_copy(k).wait_recv()
    sums = own[...]
    for k in range(1, nt):
        sums = sums + parts[k - 1]
    total[...] = sums
    grand = jnp.sum(sums, axis=1, keepdims=True)
    scaled[...] = (total[:, mine] / grand).T

    tile_lane = lax.broadcasted_iota(jnp.int32, (band, cols), 1)

    def lot_step(j, _):
        lot = lot_of(j, t)
        these = pl.ds(pl.multiple_of(lot * step_rows, step_rows), step_rows)
        for k in range(1, nt):
            mirror_copy(k, j, False).wait_recv()
        factor = scaled[these, :]
        edges = [None, None]
        for c in range(maps):
            pieces = []
            for k in range(nt):
                p = lax.rem(t + k, nt)
                at = pl.ds(pl.multiple_of(p * cols, cols), cols)
                if k:
                    sym = mirror[p, c, these, :].astype(F32) + upright[k - 1, c, these, :]
                else:
                    sym = both[c, these, :]
                pieces.append(sym - factor[:, c : c + 1] * total[c : c + 1, at])
            value = jnp.concatenate(pieces, axis=1)
            for b in range(2):
                u = 2 * lot + b
                line = value[b * band : (b + 1) * band]
                line = pltpu.roll(line, lax.rem(band + halo - u * band + width, width), 1)
                for m in range(mains):
                    corr[u, slot_of(c, m)] = line[:, m * cols : (m + 1) * cols].astype(BF)
                piece = line[:, half_w : half_w + cols]
                e = c % pack
                if e:
                    piece = pltpu.roll(piece, e * edge, 1)
                    keep = jnp.logical_and(tile_lane >= e * edge, tile_lane < (e + 1) * edge)
                    edges[b] = jnp.where(keep, piece, edges[b])
                else:
                    edges[b] = jnp.where(tile_lane < edge, piece, 0.0)
                if e == pack - 1 or c == maps - 1:
                    corr[u, slot_of(c, mains - 1) + 1] = edges[b].astype(BF)
        for b in range(2):
            u = 2 * lot + b
            head = head_of(u, t, nh)

            @pl.when(head != h)
            def _():
                @pl.when(head > h)
                def _():
                    pl.semaphore_wait(ready.at[head], 1)
                remote(corr.at[u], got.at[h], gsend, grecv, head, t).start()
        return 0

    lax.fori_loop(0, lots, lot_step, 0)
    local = pltpu.make_async_copy(corr.at[here], got.at[h], lsem)
    local.start()

    def column(line):
        return jnp.broadcast_to(line, (8, feat)).T[:, 0:1]

    for copy in load_weights:
        copy.wait()
    for layer in range(layers):
        for half in range(2):
            for v in range(2):
                for i in range(3):
                    taken = [(i, j) if v == 0 else (j, i) for j in range(3)]
                    weights[layer, half, (3 * v + i) * feat : (3 * v + i + 1) * feat, :] = jnp.concatenate(
                        [cw_ref[layer, half, dy, dx].astype(F32) for dy, dx in taken], axis=1
                    ).astype(BF)
    proj_bias = column(pb_ref[...])
    place = lax.broadcasted_iota(jnp.int32, (nh * maps, nh * slots), 1)
    for m in range(mains + pack):
        chosen = jnp.where(place == tgt_ref[:, m : m + 1], 1.0, 0.0).astype(BF)
        pwide[m * feat : (m + 1) * feat, :] = jnp.dot(
            pw_ref[...], chosen, preferred_element_type=F32
        ).astype(BF)

    def neighbour(step):
        band_there = lax.rem(spot + nd + step, nd)
        tile = band_there // nh
        return head_of(lax.rem(band_there, nh), tile, nh), tile

    up_head, up_tile = neighbour(-1)
    down_head, down_tile = neighbour(1)
    last_group = rows // halo - 1
    to_up = (
        remote(um.at[0], sm.at[0, pl.ds(halo + band, halo)], hsend.at[0], hrecv.at[0], up_head, up_tile),
        remote(ue.at[0], se.at[0, last_group], hsend.at[1], hrecv.at[1], up_head, up_tile),
    )
    to_down = (
        remote(um.at[1], sm.at[0, pl.ds(0, halo)], hsend.at[2], hrecv.at[2], down_head, down_tile),
        remote(ue.at[1], se.at[0, 0], hsend.at[3], hrecv.at[3], down_head, down_tile),
    )

    local.wait()
    rest = got.at[pl.ds(0, nh - 1)]
    pltpu.make_async_copy(rest, rest, grecv).wait()
    wide[...] = got[...].astype(F32).reshape(nh * slots * band, cols)
    lane_e = lax.broadcasted_iota(jnp.int32, (feat, cols), 1)
    for side in range(2):
        kept = sent = None
        for e in range(halo):
            r = side * halo + e
            x = wide[pl.ds(r, nh * slots, stride=band), :].astype(BF)
            value = jnp.dot(pwide[...], x, preferred_element_type=F32)
            if mains > 1:
                blocks = []
                for m in range(mains):
                    blocks.append(value[m * feat : (m + 1) * feat])
            else:
                blocks = [value[0:feat]]
            tail = value[mains * feat : (mains + 1) * feat]
            for f in range(1, pack):
                low = (mains + f) * feat
                tail = tail + jnp.where(
                    lane_e < edge, pltpu.roll(value[low : low + feat], cols - f * edge, 1), 0.0
                )
            line = jnp.concatenate(blocks + [tail], axis=1) + proj_bias
            sm[0, halo + r] = line[:, :half_w].astype(BF)
            shift = band if side == 0 else half_w + cols - band
            um[side, e] = pltpu.roll(line, shift, 1)[:, :half_w].astype(BF)
            pair = line[:, half_w - cols :]
            span = 2 * cols
            mine_at = cols - 2 * halo
            sent_at = mine_at - band if side == 0 else mine_at + band
            inside = jnp.logical_and(lane_e >= e * edge, lane_e < (e + 1) * edge)
            own_piece = pltpu.roll(pair, (span - mine_at + e * edge) % span, 1)[:, :cols]
            sent_piece = pltpu.roll(pair, (span - sent_at + e * edge) % span, 1)[:, :cols]
            kept = own_piece if kept is None else jnp.where(inside, own_piece, kept)
            sent = sent_piece if sent is None else jnp.where(inside, sent_piece, sent)
        se[0, 1 + side] = kept.astype(BF)
        ue[side] = sent.astype(BF)
        for copy in to_down if side else to_up:
            copy.start()

    first_row = spot * band - halo
    seam = lax.rem(band + halo - spot * band + width, width)
    before_seam = lax.rem(seam + width - 1, width)
    lane = lax.broadcasted_iota(jnp.int32, (feat, half_w), 1)
    lane_w = start + jnp.bitwise_and(lane_e, edge - 1)
    top_in = spot > 0
    bottom_in = spot < nd - 1

    def shifted(v, at, size):
        before = jnp.where(at == seam, 0.0, pltpu.roll(v, 1, 1))
        after = jnp.where(at == before_seam, 0.0, pltpu.roll(v, size - 1, 1))
        return before.astype(BF), v.astype(BF), after.astype(BF)

    def put(v, r, value):
        if r < halo:
            value = jnp.where(top_in, value, 0.0)
        if r >= halo + band:
            value = jnp.where(bottom_in, value, 0.0)
        for i, x in enumerate(shifted(value, lane, half_w)):
            stack[v, r, i * feat : (i + 1) * feat] = x

    def put_edge(v, g, value):
        if g == 0:
            value = jnp.where(top_in, value, 0.0)
        if g == last_group:
            value = jnp.where(bottom_in, value, 0.0)
        for i, x in enumerate(shifted(value, lane_w, cols)):
            stack_e[v, g, i * feat : (i + 1) * feat] = x

    tall = 3 * feat

    def first_taps(ref, taps_ref, r):
        block = jnp.dot(weights[0, 0], ref[0, r], preferred_element_type=F32)
        taps_ref[0, r] = block[:tall]
        taps_ref[1, r] = block[tall:]

    def begin(rr, gg):
        for r in rr:
            put(0, r, sm[0, r].astype(F32))
            first_taps(stack, taps, r)
        for g in gg:
            put_edge(0, g, se[0, g].astype(F32))
            first_taps(stack_e, taps_e, g)

    def finish(v, lines, tails):
        small = [
            pltpu.roll(line, (cols - e * edge) % cols, 1) for line in tails for e in range(pack)
        ]
        wide_main = jnp.concatenate(
            [jnp.concatenate(lines, axis=0), jnp.zeros((band, width - half_w), F32)], axis=1
        )
        wide_edge = jnp.concatenate(
            [jnp.concatenate(small, axis=0), jnp.zeros((band, width - cols), F32)], axis=1
        )
        at = lax.broadcasted_iota(jnp.int32, (band, width), 1)
        line = jnp.where(at < half_w - halo, wide_main, pltpu.roll(wide_edge, start, 1))
        line = pltpu.roll(line, lax.rem(spot * band - band - halo + width, width), 1)
        for p in range(nt):
            logits[v, p] = line[:, p * cols : (p + 1) * cols]

    readout = column(ow_ref[...])
    for layer in range(layers):
        for half in range(2):
            low = 2 * layer + half
            bias = column(cb_ref[layer, half : half + 1, :])
            if low == 0:
                begin(range(halo, halo + band), range(1, last_group))
                for copy in to_up + to_down:
                    copy.wait_recv()
                begin(range(halo), (0,))
                begin(range(halo + band, rows), (last_group,))
            else:
                for v in range(2):
                    w = weights[layer, half, v * tall : (v + 1) * tall, :]
                    for r in range(low, rows - low):
                        taps[v, r] = jnp.dot(w, stack[v, r], preferred_element_type=F32)
                    for g in range(last_group + 1):
                        taps_e[v, g] = jnp.dot(w, stack_e[v, g], preferred_element_type=F32)
            final = low == 2 * layers - 1
            came = 0 if layer == 0 else None
            for v in range(2):
                lines = []
                for s in range(low + 1, rows - low - 1):
                    conv = (
                        taps[v, s - 1, 0:feat] + taps[v, s, feat : 2 * feat]
                        + taps[v, s + 1, 2 * feat :] + bias
                    )
                    if half == 0:
                        put(v, s, jnp.where(conv > 0.0, conv, jnp.exp(jnp.minimum(conv, 0.0)) - 1.0))
                        continue
                    value = (sm[1 + v if came is None else came, s].astype(F32) + conv).astype(BF)
                    if final:
                        lines.append(jnp.sum(value.astype(F32) * readout, axis=0, keepdims=True))
                    else:
                        sm[1 + v, s] = value
                        put(v, s, value.astype(F32))
                tails = []
                for g in range(1, last_group) if final else range(last_group + 1):
                    over, under = max(g - 1, 0), min(g + 1, last_group)
                    upper = jnp.where(lane_e >= cols - edge, taps_e[v, over, 0:feat], taps_e[v, g, 0:feat])
                    lower = jnp.where(lane_e < edge, taps_e[v, under, 2 * feat :], taps_e[v, g, 2 * feat :])
                    conv = (
                        pltpu.roll(upper, edge, 1) + taps_e[v, g, feat : 2 * feat]
                        + pltpu.roll(lower, cols - edge, 1) + bias
                    )
                    if half == 0:
                        put_edge(v, g, jnp.where(conv > 0.0, conv, jnp.exp(jnp.minimum(conv, 0.0)) - 1.0))
                        continue
                    value = (se[1 + v if came is None else came, g].astype(F32) + conv).astype(BF)
                    if final:
                        tails.append(jnp.sum(value.astype(F32) * readout, axis=0, keepdims=True))
                    else:
                        se[1 + v, g] = value
                        put_edge(v, g, value.astype(F32))
                if final:
                    finish(v, lines, tails)

    owner, slot = spot // nt, lax.rem(spot, nt)

    def deliver(k):
        p = lax.rem(t + k, nt)
        return remote(
            logits.at[0, p], rows_w.at[slot], osend.at[k], orecv.at[slot], owner, p,
        )

    def turn(head):
        return logits.at[1, head * nt * band // cols]

    def wanted(col, head):
        far_off = lax.rem(col - head * nt + nd, nd)
        return jnp.logical_or(far_off > nd // 2, lax.rem(far_off - (nt - 1) + nd, nd) > nd // 2)

    def send_turned(i, _):
        head = lax.rem(h + i, nh)

        @pl.when(wanted(spot, head))
        def _():
            remote(
                turn(head), rows_t.at[here], tsend.at[head], trecv.at[here], head, t
            ).start()
        return 0

    for k in range(1, nt):
        deliver(k).start()
    lax.fori_loop(1, nh, send_turned, 0)

    @pl.when(owner == h)
    def _():
        pltpu.make_async_copy(logits.at[0, t], rows_w.at[slot], orecv.at[slot]).start()

    @pl.when(owner != h)
    def _():
        deliver(0).start()

    rows_t[here] = logits[1, h * nt * band // cols]
    one = rows_t.at[0]

    def await_piece(i, _):
        @pl.when(jnp.logical_and(i != here, wanted(t * nh + i, h)))
        def _():
            pltpu.make_async_copy(one, one, trecv.at[i]).wait()
        return 0

    lax.fori_loop(0, nh, await_piece, 0)
    turned[...] = rows_t[...].reshape(nh * band, cols).T
    for k in range(nt):
        pltpu.make_async_copy(logits.at[0, k], rows_w.at[k], orecv.at[k]).wait()
    block = turned[pl.ds(pl.multiple_of(lax.rem(h * nt * band, cols), nt * band), nt * band), :]
    shape = (nt, band, cols)
    row_band = h * nt + lax.broadcasted_iota(jnp.int32, shape, 0)
    col_band = t * nh + jnp.right_shift(lax.broadcasted_iota(jnp.int32, shape, 2), band.bit_length() - 1)
    away = col_band - row_band
    away = jnp.where(away < 0, away + nd, away)
    out_ref[...] = jnp.where(away <= nd // 2, rows_w[...], block.reshape(shape))

    @pl.when(owner != h)
    def _():
        deliver(0).wait_send()

    for k in range(1, nt):
        deliver(k).wait_send()
        parts_copy(k).wait_send()
        for j in range(lots):
            mirror_copy(k, j, True).wait_send()
    for copy in to_up + to_down:
        copy.wait_send()
    pltpu.make_async_copy(rest, rest, gsend).wait()

    def sent(i, _):
        head = lax.rem(h + i, nh)

        @pl.when(wanted(spot, head))
        def _():
            pltpu.make_async_copy(one, one, tsend.at[head]).wait()
        return 0

    lax.fori_loop(1, nh, sent, 0)


def on_device(attention, proj_weight, proj_bias, conv_weight, conv_bias, out_weight):
    nh, nt = lax.axis_size("head"), lax.axis_size("tile")
    nd = nh * nt
    maps, width, cols = attention.shape
    layers, two, feat = conv_weight.shape[:3]
    band = width // nd
    far = max(nt - 1, 1)
    halo = 2 * layers
    rows = band + 2 * halo
    half_w = width // 2
    mains = half_w // cols
    pack = cols // (3 * band + 2 * halo)
    assert pack == halo and band == 2 * halo and nh * band == cols
    groups = [range(g, min(g + pack, maps)) for g in range(0, maps, pack)]
    slots = maps * mains + len(groups)
    count = rows // halo
    ordered = jnp.transpose(conv_weight, (0, 1, 4, 5, 2, 3))
    target = np.full((nh * maps, mains + pack), -1, np.int32)
    for src in range(nh):
        for c in range(maps):
            g = c // pack
            for m in range(mains):
                target[src * maps + c, m] = src * slots + c * mains + m + g
            target[src * maps + c, mains + c % pack] = src * slots + groups[g].stop * mains + g
    dma = pltpu.SemaphoreType.DMA
    out = pl.pallas_call(
        functools.partial(kernel, nh, nt),
        out_shape=jax.ShapeDtypeStruct((nt, band, cols), F32),
        in_specs=[pl.BlockSpec(memory_space=pltpu.HBM)] * 7,
        out_specs=pl.BlockSpec(memory_space=VM),
        scratch_shapes=[
            VM((maps, width, cols), BF),
            VM(proj_weight.shape, BF),
            VM((1, feat), F32),
            VM(ordered.shape, BF),
            VM(conv_bias.shape, F32),
            VM((1, feat), F32),
            VM(target.shape, jnp.int32),
            VM((nt, maps, cols, cols), BF),
            VM((maps, cols, cols), F32),
            VM((far, maps, cols, cols), F32),
            VM((cols, maps), F32),
            VM((maps, width), F32),
            VM((maps, width), F32),
            VM((far, maps, width), F32),
            VM((nh, slots, band, cols), BF),
            VM((nh, slots, band, cols), BF),
            VM((nh * slots * band, cols), F32),
            VM(((mains + pack) * feat, nh * slots), BF),
            VM((layers, two, 6 * feat, 3 * feat), BF),
            VM((3, rows, feat, half_w), BF),
            VM((3, count, feat, cols), BF),
            VM((2, halo, feat, half_w), BF),
            VM((2, feat, cols), BF),
            VM((2, rows, 3 * feat, half_w), BF),
            VM((2, count, 3 * feat, cols), BF),
            VM((2, rows, 3 * feat, half_w), F32),
            VM((2, count, 3 * feat, cols), F32),
            VM((2, nt, band, cols), F32),
            VM((nt, band, cols), F32),
            VM((nh, band, cols), F32),
            VM((cols, cols), F32),
            dma,
            dma((6,)),
            dma((far, nh // 2)),
            dma((far, nh // 2)),
            dma((far,)),
            dma((far,)),
            dma,
            dma,
            dma,
            dma((4,)),
            dma((4,)),
            dma((nt,)),
            dma((nt,)),
            dma((nh,)),
            dma((nh,)),
            pltpu.SemaphoreType.REGULAR((nh,)),
        ],
        compiler_params=pltpu.CompilerParams(
            collective_id=0, has_side_effects=True, vmem_limit_bytes=56 * 1024 * 1024
        ),
        name="head",
    )(
        attention, proj_weight, proj_bias[None], ordered, conv_bias, out_weight[None], target,
    )
    return out.reshape(nt * band, cols)


def solution(mesh):
    return jax.shard_map(
        on_device,
        mesh=mesh,
        in_specs=(P(("grp", "head"), None, "tile"), P(), P(), P(), P(), P()),
        out_specs=P(("grp", "head"), "tile"),
        check_vma=False,
    )
```

```python
import functools
import jax
import jax.numpy as jnp
import numpy as np
from jax import lax
from jax.experimental import pallas as pl
from jax.experimental.pallas import tpu as pltpu
from jax.sharding import PartitionSpec as P

VM = pltpu.VMEM
BF = jnp.bfloat16
F32 = jnp.float32
MESH = pl.DeviceIdType.MESH


def remote(src, dst, send, recv, head, tile):
    return pltpu.make_async_remote_copy(
        src_ref=src,
        dst_ref=dst,
        send_sem=send,
        recv_sem=recv,
        device_id={"head": head, "tile": tile},
        device_id_type=MESH,
    )


def fold(head):
    pair, core = head // 2, lax.rem(head, 2)
    row, col = pair // 2, lax.rem(pair, 2)
    col = jnp.where(lax.rem(row, 2) == 0, col, 1 - col)
    return (row * 2 + col) * 2 + core


def spot_of(head, tile, nh):
    place = fold(head)
    return jnp.where(lax.rem(tile, 2) == 0, place, nh - 1 - place)


def head_of(spot, tile, nh):
    return fold(jnp.where(lax.rem(tile, 2) == 0, spot, nh - 1 - spot))


def kernel(
    nh, nt, a_hbm, pw_hbm, pb_hbm, cw_hbm, cb_hbm, ow_hbm, tgt_hbm, out_ref,
    a_ref, pw_ref, pb_ref, cw_ref, cb_ref, ow_ref, tgt_ref, mirror, both, upright, scaled, own, total, parts, corr, got, wide, pwide, weights,
    sm, se, um, ue, stack, stack_e, taps, taps_e, final_rows, logits, rows_w, rows_t, turned,
    asem, wsem, msend, mrecv, psend, precv, gsend, grecv, lsem,
    hsend, hrecv, osend, orecv, tsend, trecv, ready,
):
    maps, width, cols = a_ref.shape
    slots, band = got.shape[1:3]
    nd = nh * nt
    half_w = width // 2
    mains = half_w // cols
    feat = pw_ref.shape[0]
    layers = cw_ref.shape[0]
    halo = 2 * layers
    rows = band + 2 * halo
    edge = 3 * band + 2 * halo
    pack = cols // edge
    start = half_w - 2 * halo
    h = lax.axis_index("head")
    t = lax.axis_index("tile")
    here = spot_of(h, t, nh)
    spot = t * nh + here

    def slot_of(c, m=0):
        return c * mains + m + c // pack

    load = pltpu.make_async_copy(a_hbm, a_ref, asem)
    load.start()
    barrier = pltpu.get_barrier_semaphore()

    def greet(head, tile):
        pl.semaphore_signal(
            barrier, inc=1, device_id={"head": head, "tile": tile}, device_id_type=MESH
        )

    for k in range(1, nt):
        greet(h, lax.rem(t + k, nt))

    def greet_later(i, _):
        greet(i, t)
        return 0

    lax.fori_loop(h + 1, nh, greet_later, 0)
    load_weights = [
        pltpu.make_async_copy(src, dst, wsem.at[i])
        for i, (src, dst) in enumerate((
            (cw_hbm, cw_ref), (pw_hbm, pw_ref), (pb_hbm, pb_ref), (cb_hbm, cb_ref), (ow_hbm, ow_ref),
            (tgt_hbm, tgt_ref),
        ))
    ]
    for copy in load_weights:
        copy.start()
    pl.semaphore_wait(barrier, nt - 1 + h)

    def tell_earlier(i, _):
        pl.semaphore_signal(
            ready.at[h], inc=1, device_id={"head": i, "tile": t}, device_id_type=MESH
        )
        return 0

    lots = nh // 2
    step_rows = 2 * band

    def lot_of(j, tile):
        other = (h < nh // 2) == (lax.rem(tile, 2) == 0)
        return lax.rem(j + jnp.where(other, lots // 2, 0), lots)

    def mirror_copy(k, j, to):
        p = lax.rem(t + k, nt)
        low = pl.multiple_of(lot_of(j, p if to else t) * step_rows, step_rows)
        return remote(
            a_hbm.at[:, pl.ds(pl.multiple_of(p * cols + low, step_rows), step_rows), :],
            mirror.at[t, :, pl.ds(low, step_rows)],
            msend.at[k - 1, j], mrecv.at[k - 1, j], h, p,
        )

    def parts_copy(k):
        p = lax.rem(t + k, nt)
        return remote(own, parts.at[k - 1], psend.at[k - 1], precv.at[k - 1], h, p)

    for k in range(1, nt):
        mirror_copy(k, 0, True).start()
    lax.fori_loop(0, h, tell_earlier, 0)

    load.wait()
    mine = pl.ds(pl.multiple_of(t * cols, cols), cols)
    ones_t = jnp.ones((8, cols), BF)
    ones_w = jnp.ones((8, width), BF)
    for c in range(maps):
        a = a_ref[c]
        line = lax.dot_general(ones_t, a, (((1,), (1,)), ((), ())), preferred_element_type=F32)
        own[c : c + 1, :] = line[0:1]
        columns = jnp.dot(ones_w, a, preferred_element_type=F32)
        own[c : c + 1, mine] = own[c : c + 1, mine] + columns[0:1]
    for k in range(1, nt):
        parts_copy(k).start()
    for k in range(1, nt):
        for j in range(1, lots):
            mirror_copy(k, j, True).start()
    for c in range(maps):
        a = a_ref[c, mine, :].astype(F32)
        both[c] = a + a.T
        for k in range(1, nt):
            at = pl.ds(pl.multiple_of(lax.rem(t + k, nt) * cols, cols), cols)
            upright[k - 1, c] = a_ref[c, at, :].astype(F32).T
    for k in range(1, nt):
        parts_copy(k).wait_recv()
    sums = own[...]
    for k in range(1, nt):
        sums = sums + parts[k - 1]
    total[...] = sums
    grand = jnp.sum(sums, axis=1, keepdims=True)
    scaled[...] = (total[:, mine] / grand).T

    tile_lane = lax.broadcasted_iota(jnp.int32, (band, cols), 1)

    def lot_step(j, _):
        lot = lot_of(j, t)
        these = pl.ds(pl.multiple_of(lot * step_rows, step_rows), step_rows)
        for k in range(1, nt):
            mirror_copy(k, j, False).wait_recv()
        factor = scaled[these, :]
        edges = [None, None]
        for c in range(maps):
            pieces = []
            for k in range(nt):
                p = lax.rem(t + k, nt)
                at = pl.ds(pl.multiple_of(p * cols, cols), cols)
                if k:
                    sym = mirror[p, c, these, :].astype(F32) + upright[k - 1, c, these, :]
                else:
                    sym = both[c, these, :]
                pieces.append(sym - factor[:, c : c + 1] * total[c : c + 1, at])
            value = jnp.concatenate(pieces, axis=1)
            for b in range(2):
                u = 2 * lot + b
                line = value[b * band : (b + 1) * band]
                line = pltpu.roll(line, lax.rem(band + halo - u * band + width, width), 1)
                for m in range(mains):
                    corr[u, slot_of(c, m)] = line[:, m * cols : (m + 1) * cols].astype(BF)
                piece = line[:, half_w : half_w + cols]
                e = c % pack
                if e:
                    piece = pltpu.roll(piece, e * edge, 1)
                    keep = jnp.logical_and(tile_lane >= e * edge, tile_lane < (e + 1) * edge)
                    edges[b] = jnp.where(keep, piece, edges[b])
                else:
                    edges[b] = jnp.where(tile_lane < edge, piece, 0.0)
                if e == pack - 1 or c == maps - 1:
                    corr[u, slot_of(c, mains - 1) + 1] = edges[b].astype(BF)
        for b in range(2):
            u = 2 * lot + b
            head = head_of(u, t, nh)

            @pl.when(head != h)
            def _():
                @pl.when(head > h)
                def _():
                    pl.semaphore_wait(ready.at[head], 1)
                remote(corr.at[u], got.at[h], gsend, grecv, head, t).start()
        return 0

    lax.fori_loop(0, lots, lot_step, 0)
    local = pltpu.make_async_copy(corr.at[here], got.at[h], lsem)
    local.start()

    def column(line):
        return jnp.broadcast_to(line, (8, feat)).T[:, 0:1]

    for copy in load_weights:
        copy.wait()
    for layer in range(layers):
        for half in range(2):
            for v in range(2):
                for i in range(3):
                    taken = [(i, j) if v == 0 else (j, i) for j in range(3)]
                    weights[layer, half, (3 * v + i) * feat : (3 * v + i + 1) * feat, :] = jnp.concatenate(
                        [cw_ref[layer, half, dy, dx].astype(F32) for dy, dx in taken], axis=1
                    ).astype(BF)
    proj_bias = column(pb_ref[...])
    place = lax.broadcasted_iota(jnp.int32, (nh * maps, nh * slots), 1)
    for m in range(mains + pack):
        chosen = jnp.where(place == tgt_ref[:, m : m + 1], 1.0, 0.0).astype(BF)
        pwide[m * feat : (m + 1) * feat, :] = jnp.dot(
            pw_ref[...], chosen, preferred_element_type=F32
        ).astype(BF)

    def neighbour(step):
        band_there = lax.rem(spot + nd + step, nd)
        tile = band_there // nh
        return head_of(lax.rem(band_there, nh), tile, nh), tile

    up_head, up_tile = neighbour(-1)
    down_head, down_tile = neighbour(1)
    last_group = rows // halo - 1
    def halo_copies(side):
        up = side == 0
        there = (jnp.where(up, up_head, down_head), jnp.where(up, up_tile, down_tile))
        rows_there = sm.at[0, pl.ds(jnp.where(up, halo + band, 0), halo)]
        edge_there = se.at[0, jnp.where(up, last_group, 0)]
        return (
            remote(um.at[side], rows_there, hsend.at[2 * side], hrecv.at[2 * side], *there),
            remote(ue.at[side], edge_there, hsend.at[2 * side + 1], hrecv.at[2 * side + 1], *there),
        )

    local.wait()
    rest = got.at[pl.ds(0, nh - 1)]
    pltpu.make_async_copy(rest, rest, grecv).wait()
    wide[...] = got[...].astype(F32).reshape(nh * slots * band, cols)
    lane_e = lax.broadcasted_iota(jnp.int32, (feat, cols), 1)
    for i in range(2):
        side = lax.rem(spot + i, 2)
        kept = sent = None
        for e in range(halo):
            r = side * halo + e
            x = wide[pl.ds(r, nh * slots, stride=band), :].astype(BF)
            value = jnp.dot(pwide[...], x, preferred_element_type=F32)
            if mains > 1:
                blocks = []
                for m in range(mains):
                    blocks.append(value[m * feat : (m + 1) * feat])
            else:
                blocks = [value[0:feat]]
            tail = value[mains * feat : (mains + 1) * feat]
            for f in range(1, pack):
                low = (mains + f) * feat
                tail = tail + jnp.where(
                    lane_e < edge, pltpu.roll(value[low : low + feat], cols - f * edge, 1), 0.0
                )
            line = jnp.concatenate(blocks + [tail], axis=1) + proj_bias
            sm[0, halo + r] = line[:, :half_w].astype(BF)
            shift = jnp.where(side == 0, band, half_w + cols - band)
            um[side, e] = pltpu.roll(line, shift, 1)[:, :half_w].astype(BF)
            pair = line[:, half_w - cols :]
            span = 2 * cols
            mine_at = cols - 2 * halo
            sent_at = jnp.where(side == 0, mine_at - band, mine_at + band)
            inside = jnp.logical_and(lane_e >= e * edge, lane_e < (e + 1) * edge)
            own_piece = pltpu.roll(pair, (span - mine_at + e * edge) % span, 1)[:, :cols]
            sent_piece = pltpu.roll(pair, lax.rem(span - sent_at + e * edge, span), 1)[:, :cols]
            kept = own_piece if kept is None else jnp.where(inside, own_piece, kept)
            sent = sent_piece if sent is None else jnp.where(inside, sent_piece, sent)
        se[0, 1 + side] = kept.astype(BF)
        ue[side] = sent.astype(BF)
        for copy in halo_copies(side):
            copy.start()

    first_row = spot * band - halo
    seam = lax.rem(band + halo - spot * band + width, width)
    before_seam = lax.rem(seam + width - 1, width)
    lane = lax.broadcasted_iota(jnp.int32, (feat, half_w), 1)
    lane_w = start + jnp.bitwise_and(lane_e, edge - 1)
    top_in = spot > 0
    bottom_in = spot < nd - 1

    def shifted(v, at, size):
        before = jnp.where(at == seam, 0.0, pltpu.roll(v, 1, 1))
        after = jnp.where(at == before_seam, 0.0, pltpu.roll(v, size - 1, 1))
        return before.astype(BF), v.astype(BF), after.astype(BF)

    def put(v, r, value, inside=None):
        if inside is not None:
            value = jnp.where(inside, value, 0.0)
        for i, x in enumerate(shifted(value, lane, half_w)):
            stack[v, r, i * feat : (i + 1) * feat] = x

    def put_edge(v, g, value):
        if g == 0:
            value = jnp.where(top_in, value, 0.0)
        if g == last_group:
            value = jnp.where(bottom_in, value, 0.0)
        for i, x in enumerate(shifted(value, lane_w, cols)):
            stack_e[v, g, i * feat : (i + 1) * feat] = x

    tall = 3 * feat

    def finish(v, tails):
        small = [
            pltpu.roll(line, (cols - e * edge) % cols, 1) for line in tails for e in range(pack)
        ]
        wide_main = jnp.concatenate(
            [final_rows[v], jnp.zeros((band, width - half_w), F32)], axis=1
        )
        wide_edge = jnp.concatenate(
            [jnp.concatenate(small, axis=0), jnp.zeros((band, width - cols), F32)], axis=1
        )
        at = lax.broadcasted_iota(jnp.int32, (band, width), 1)
        line = jnp.where(at < half_w - halo, wide_main, pltpu.roll(wide_edge, start, 1))
        line = pltpu.roll(line, lax.rem(spot * band - band - halo + width, width), 1)
        for p in range(nt):
            logits[v, p] = line[:, p * cols : (p + 1) * cols]

    readout = column(ow_ref[...])
    biases = [column(cb_ref[low // 2, low % 2 : low % 2 + 1, :]) for low in range(2 * layers)]
    last = 2 * layers - 1

    def weight(low, v):
        return weights[low // 2, low % 2, v * tall : (v + 1) * tall, :]

    def elu(x):
        return jnp.where(x > 0.0, x, jnp.exp(jnp.minimum(x, 0.0)) - 1.0)

    def product(low, source, store, these):
        for n in range(0, len(these), 2):
            two = these[n : n + 2]
            for v in range(1 if low == 0 else 2):
                x = jnp.concatenate([source[v, r] for r in two], axis=1)
                w = weights[0, 0] if low == 0 else weight(low, v)
                block = jnp.dot(w, x, preferred_element_type=F32)
                size = block.shape[1] // len(two)
                for i, r in enumerate(two):
                    got_r = block[:, i * size : (i + 1) * size]
                    if low == 0:
                        store(0, r, got_r[:tall])
                        store(1, r, got_r[tall:])
                    else:
                        store(v, r, got_r)

    def multiply(low, these, inside=None):
        if low == 0:
            for r in these:
                put(0, r, sm[0, r].astype(F32), inside and inside(r))

        def store(v, r, x):
            taps[low % 2, v, r] = x

        product(low, stack, store, these)

    def gather(low, s, inside=None):
        for v in range(2):
            part = taps.at[low % 2, v]
            conv = part[s - 1, 0:feat] + part[s, feat : 2 * feat] + part[s + 1, 2 * feat :] + biases[low]
            if low % 2 == 0:
                put(v, s, elu(conv), inside)
                continue
            value = (sm[0 if low == 1 else 1 + v, s].astype(F32) + conv).astype(BF)
            if low < last:
                sm[1 + v, s] = value
                put(v, s, value.astype(F32), inside)
            else:
                final_rows[v, pl.ds(s - halo, 1), :] = jnp.sum(
                    value.astype(F32) * readout, axis=0, keepdims=True
                )

    def multiply_edges(low):
        these = list(range(last_group + 1))
        if low == 0:
            for g in these:
                put_edge(0, g, se[0, g].astype(F32))

        def store(v, g, x):
            taps_e[v, g] = x

        product(low, stack_e, store, these)

    def gather_edges(low):
        for v in range(2):
            tails = []
            for g in range(1, last_group) if low == last else range(last_group + 1):
                over, under = max(g - 1, 0), min(g + 1, last_group)
                upper = jnp.where(lane_e >= cols - edge, taps_e[v, over, 0:feat], taps_e[v, g, 0:feat])
                lower = jnp.where(lane_e < edge, taps_e[v, under, 2 * feat :], taps_e[v, g, 2 * feat :])
                conv = (
                    pltpu.roll(upper, edge, 1) + taps_e[v, g, feat : 2 * feat]
                    + pltpu.roll(lower, cols - edge, 1) + biases[low]
                )
                if low % 2 == 0:
                    put_edge(v, g, elu(conv))
                    continue
                value = (se[0 if low == 1 else 1 + v, g].astype(F32) + conv).astype(BF)
                if low < last:
                    se[1 + v, g] = value
                    put_edge(v, g, value.astype(F32))
                else:
                    tails.append(jnp.sum(value.astype(F32) * readout, axis=0, keepdims=True))
            if low == last:
                finish(v, tails)

    for low in range(2 * layers):
        early = range(halo + low, halo + band - low)
        multiply(low, list(early))
        for s in early[1:-1]:
            gather(low, s)

    def await_halo(below):
        fringe = sm.at[0, pl.ds(halo + band if below else 0, halo)]
        corner = se.at[0, last_group if below else 0]
        came = 0 if below else 2
        pltpu.make_async_copy(fringe, fringe, hrecv.at[came]).wait()
        pltpu.make_async_copy(corner, corner, hrecv.at[came + 1]).wait()

    def inside(r):
        if r < halo:
            return top_in
        return bottom_in if r >= halo + band else None

    def late():
        for low in range(2 * layers):
            these = [r for n in range(low, halo + low) for r in (n, rows - 1 - n)]
            multiply(low, these, inside)
            multiply_edges(low)
            for n in range(low + 1, halo + low + 1):
                for s in (n, rows - 1 - n):
                    gather(low, s, inside(s))
            gather_edges(low)

    for below in (False, True):
        await_halo(below)
    late()

    owner, slot = spot // nt, lax.rem(spot, nt)

    def deliver(k):
        p = lax.rem(t + k, nt)
        return remote(
            logits.at[0, p], rows_w.at[slot], osend.at[k], orecv.at[slot], owner, p,
        )

    def turn(head):
        return logits.at[1, head * nt * band // cols]

    def wanted(col, head):
        far_off = lax.rem(col - head * nt + nd, nd)
        return jnp.logical_or(far_off > nd // 2, lax.rem(far_off - (nt - 1) + nd, nd) > nd // 2)

    def send_turned(i, _):
        head = lax.rem(h + i, nh)

        @pl.when(wanted(spot, head))
        def _():
            remote(
                turn(head), rows_t.at[here], tsend.at[head], trecv.at[here], head, t
            ).start()
        return 0

    for k in range(1, nt):
        deliver(k).start()
    lax.fori_loop(1, nh, send_turned, 0)

    @pl.when(owner == h)
    def _():
        pltpu.make_async_copy(logits.at[0, t], rows_w.at[slot], orecv.at[slot]).start()

    @pl.when(owner != h)
    def _():
        deliver(0).start()

    rows_t[here] = logits[1, h * nt * band // cols]
    one = rows_t.at[0]

    def await_piece(i, _):
        @pl.when(jnp.logical_and(i != here, wanted(t * nh + i, h)))
        def _():
            pltpu.make_async_copy(one, one, trecv.at[i]).wait()
        return 0

    lax.fori_loop(0, nh, await_piece, 0)
    turned[...] = rows_t[...].reshape(nh * band, cols).T
    for k in range(nt):
        pltpu.make_async_copy(logits.at[0, k], rows_w.at[k], orecv.at[k]).wait()
    block = turned[pl.ds(pl.multiple_of(lax.rem(h * nt * band, cols), nt * band), nt * band), :]
    shape = (nt, band, cols)
    row_band = h * nt + lax.broadcasted_iota(jnp.int32, shape, 0)
    col_band = t * nh + jnp.right_shift(lax.broadcasted_iota(jnp.int32, shape, 2), band.bit_length() - 1)
    away = col_band - row_band
    away = jnp.where(away < 0, away + nd, away)
    out_ref[...] = jnp.where(away <= nd // 2, rows_w[...], block.reshape(shape))

    @pl.when(owner != h)
    def _():
        deliver(0).wait_send()

    for k in range(1, nt):
        deliver(k).wait_send()
        parts_copy(k).wait_send()
        for j in range(lots):
            mirror_copy(k, j, True).wait_send()
    for side in range(2):
        for copy in halo_copies(side):
            copy.wait_send()
    pltpu.make_async_copy(rest, rest, gsend).wait()

    def sent(i, _):
        head = lax.rem(h + i, nh)

        @pl.when(wanted(spot, head))
        def _():
            pltpu.make_async_copy(one, one, tsend.at[head]).wait()
        return 0

    lax.fori_loop(1, nh, sent, 0)


def on_device(attention, proj_weight, proj_bias, conv_weight, conv_bias, out_weight):
    nh, nt = lax.axis_size("head"), lax.axis_size("tile")
    nd = nh * nt
    maps, width, cols = attention.shape
    layers, two, feat = conv_weight.shape[:3]
    band = width // nd
    far = max(nt - 1, 1)
    halo = 2 * layers
    rows = band + 2 * halo
    half_w = width // 2
    mains = half_w // cols
    pack = cols // (3 * band + 2 * halo)
    assert pack == halo and band == 2 * halo and nh * band == cols
    groups = [range(g, min(g + pack, maps)) for g in range(0, maps, pack)]
    slots = maps * mains + len(groups)
    count = rows // halo
    ordered = jnp.transpose(conv_weight, (0, 1, 4, 5, 2, 3))
    target = np.full((nh * maps, mains + pack), -1, np.int32)
    for src in range(nh):
        for c in range(maps):
            g = c // pack
            for m in range(mains):
                target[src * maps + c, m] = src * slots + c * mains + m + g
            target[src * maps + c, mains + c % pack] = src * slots + groups[g].stop * mains + g
    dma = pltpu.SemaphoreType.DMA
    out = pl.pallas_call(
        functools.partial(kernel, nh, nt),
        out_shape=jax.ShapeDtypeStruct((nt, band, cols), F32),
        in_specs=[pl.BlockSpec(memory_space=pltpu.HBM)] * 7,
        out_specs=pl.BlockSpec(memory_space=VM),
        scratch_shapes=[
            VM((maps, width, cols), BF),
            VM(proj_weight.shape, BF),
            VM((1, feat), F32),
            VM(ordered.shape, BF),
            VM(conv_bias.shape, F32),
            VM((1, feat), F32),
            VM(target.shape, jnp.int32),
            VM((nt, maps, cols, cols), BF),
            VM((maps, cols, cols), F32),
            VM((far, maps, cols, cols), F32),
            VM((cols, maps), F32),
            VM((maps, width), F32),
            VM((maps, width), F32),
            VM((far, maps, width), F32),
            VM((nh, slots, band, cols), BF),
            VM((nh, slots, band, cols), BF),
            VM((nh * slots * band, cols), F32),
            VM(((mains + pack) * feat, nh * slots), BF),
            VM((layers, two, 6 * feat, 3 * feat), BF),
            VM((3, rows, feat, half_w), BF),
            VM((3, count, feat, cols), BF),
            VM((2, halo, feat, half_w), BF),
            VM((2, feat, cols), BF),
            VM((2, rows, 3 * feat, half_w), BF),
            VM((2, count, 3 * feat, cols), BF),
            VM((2, 2, rows, 3 * feat, half_w), F32),
            VM((2, count, 3 * feat, cols), F32),
            VM((2, band, half_w), F32),
            VM((2, nt, band, cols), F32),
            VM((nt, band, cols), F32),
            VM((nh, band, cols), F32),
            VM((cols, cols), F32),
            dma,
            dma((6,)),
            dma((far, nh // 2)),
            dma((far, nh // 2)),
            dma((far,)),
            dma((far,)),
            dma,
            dma,
            dma,
            dma((4,)),
            dma((4,)),
            dma((nt,)),
            dma((nt,)),
            dma((nh,)),
            dma((nh,)),
            pltpu.SemaphoreType.REGULAR((nh,)),
        ],
        compiler_params=pltpu.CompilerParams(
            collective_id=0, has_side_effects=True, vmem_limit_bytes=55200 * 1024
        ),
        name="head",
    )(
        attention, proj_weight, proj_bias[None], ordered, conv_bias, out_weight[None], target,
    )
    return out.reshape(nt * band, cols)


def solution(mesh):
    return jax.shard_map(
        on_device,
        mesh=mesh,
        in_specs=(P(("grp", "head"), None, "tile"), P(), P(), P(), P(), P()),
        out_specs=P(("grp", "head"), "tile"),
        check_vma=False,
    )
```

```python
import functools
import jax
import jax.numpy as jnp
import numpy as np
from jax import lax
from jax.experimental import pallas as pl
from jax.experimental.pallas import tpu as pltpu
from jax.sharding import PartitionSpec as P

VM = pltpu.VMEM
BF = jnp.bfloat16
F32 = jnp.float32
MESH = pl.DeviceIdType.MESH


def remote(src, dst, send, recv, head, tile):
    return pltpu.make_async_remote_copy(
        src_ref=src,
        dst_ref=dst,
        send_sem=send,
        recv_sem=recv,
        device_id={"head": head, "tile": tile},
        device_id_type=MESH,
    )


def fold(head):
    pair, core = head // 2, lax.rem(head, 2)
    row, col = pair // 2, lax.rem(pair, 2)
    col = jnp.where(lax.rem(row, 2) == 0, col, 1 - col)
    return (row * 2 + col) * 2 + core


def spot_of(head, tile, nh):
    place = fold(head)
    return jnp.where(lax.rem(tile, 2) == 0, place, nh - 1 - place)


def head_of(spot, tile, nh):
    return fold(jnp.where(lax.rem(tile, 2) == 0, spot, nh - 1 - spot))


def kernel(
    nh, nt, a_hbm, pw_hbm, pb_hbm, cw_hbm, cb_hbm, ow_hbm, tgt_hbm, out_ref,
    a_ref, pw_ref, pb_ref, cw_ref, cb_ref, ow_ref, tgt_ref, mirror, both, upright, scaled, own, total, parts, corr, got, wide, pwide, weights,
    sm, se, um, ue, stack, stack_e, taps, taps_e, final_rows, logits, rows_w, rows_t, turned,
    asem, wsem, msend, mrecv, psend, precv, gsend, grecv, lsem,
    hsend, hrecv, osend, orecv, tsend, trecv, ready,
):
    maps, width, cols = a_ref.shape
    slots, band = got.shape[1:3]
    nd = nh * nt
    half_w = width // 2
    mains = half_w // cols
    feat = pw_ref.shape[0]
    layers = cw_ref.shape[0]
    halo = 2 * layers
    rows = band + 2 * halo
    edge = 3 * band + 2 * halo
    pack = cols // edge
    start = half_w - 2 * halo
    h = lax.axis_index("head")
    t = lax.axis_index("tile")
    here = spot_of(h, t, nh)
    spot = t * nh + here

    def slot_of(c, m=0):
        return c * mains + m + c // pack

    load = pltpu.make_async_copy(a_hbm, a_ref, asem)
    load.start()
    barrier = pltpu.get_barrier_semaphore()

    def greet(head, tile):
        pl.semaphore_signal(
            barrier, inc=1, device_id={"head": head, "tile": tile}, device_id_type=MESH
        )

    for k in range(1, nt):
        greet(h, lax.rem(t + k, nt))

    def greet_later(i, _):
        greet(i, t)
        return 0

    lax.fori_loop(h + 1, nh, greet_later, 0)
    load_weights = [
        pltpu.make_async_copy(src, dst, wsem.at[i])
        for i, (src, dst) in enumerate((
            (cw_hbm, cw_ref), (pw_hbm, pw_ref), (pb_hbm, pb_ref), (cb_hbm, cb_ref), (ow_hbm, ow_ref),
            (tgt_hbm, tgt_ref),
        ))
    ]
    for copy in load_weights:
        copy.start()
    pl.semaphore_wait(barrier, nt - 1 + h)

    def tell_earlier(i, _):
        pl.semaphore_signal(
            ready.at[h], inc=1, device_id={"head": i, "tile": t}, device_id_type=MESH
        )
        return 0

    lots = nh // 2
    step_rows = 2 * band

    def lot_of(j, tile):
        other = (h < nh // 2) == (lax.rem(tile, 2) == 0)
        return lax.rem(j + jnp.where(other, lots // 2, 0), lots)

    def mirror_copy(k, j, to):
        p = lax.rem(t + k, nt)
        low = pl.multiple_of(lot_of(j, p if to else t) * step_rows, step_rows)
        return remote(
            a_hbm.at[:, pl.ds(pl.multiple_of(p * cols + low, step_rows), step_rows), :],
            mirror.at[t, :, pl.ds(low, step_rows)],
            msend.at[k - 1, j], mrecv.at[k - 1, j], h, p,
        )

    def parts_copy(k):
        p = lax.rem(t + k, nt)
        return remote(own, parts.at[k - 1], psend.at[k - 1], precv.at[k - 1], h, p)

    for k in range(1, nt):
        mirror_copy(k, 0, True).start()
    lax.fori_loop(0, h, tell_earlier, 0)

    load.wait()
    mine = pl.ds(pl.multiple_of(t * cols, cols), cols)
    ones_t = jnp.ones((8, cols), BF)
    ones_w = jnp.ones((8, width), BF)
    for c in range(maps):
        a = a_ref[c]
        line = lax.dot_general(ones_t, a, (((1,), (1,)), ((), ())), preferred_element_type=F32)
        own[c : c + 1, :] = line[0:1]
        columns = jnp.dot(ones_w, a, preferred_element_type=F32)
        own[c : c + 1, mine] = own[c : c + 1, mine] + columns[0:1]
    for k in range(1, nt):
        parts_copy(k).start()
    for k in range(1, nt):
        for j in range(1, lots):
            mirror_copy(k, j, True).start()
    for c in range(maps):
        a = a_ref[c, mine, :].astype(F32)
        both[c] = a + a.T
        for k in range(1, nt):
            at = pl.ds(pl.multiple_of(lax.rem(t + k, nt) * cols, cols), cols)
            upright[k - 1, c] = a_ref[c, at, :].astype(F32).T
    for k in range(1, nt):
        parts_copy(k).wait_recv()
    sums = own[...]
    for k in range(1, nt):
        sums = sums + parts[k - 1]
    total[...] = sums
    grand = jnp.sum(sums, axis=1, keepdims=True)
    scaled[...] = (total[:, mine] / grand).T

    tile_lane = lax.broadcasted_iota(jnp.int32, (band, cols), 1)

    def lot_step(j, _):
        lot = lot_of(j, t)
        these = pl.ds(pl.multiple_of(lot * step_rows, step_rows), step_rows)
        for k in range(1, nt):
            mirror_copy(k, j, False).wait_recv()
        factor = scaled[these, :]
        edges = [None, None]
        for c in range(maps):
            pieces = []
            for k in range(nt):
                p = lax.rem(t + k, nt)
                at = pl.ds(pl.multiple_of(p * cols, cols), cols)
                if k:
                    sym = mirror[p, c, these, :].astype(F32) + upright[k - 1, c, these, :]
                else:
                    sym = both[c, these, :]
                pieces.append(sym - factor[:, c : c + 1] * total[c : c + 1, at])
            value = jnp.concatenate(pieces, axis=1)
            for b in range(2):
                u = 2 * lot + b
                line = value[b * band : (b + 1) * band]
                line = pltpu.roll(line, lax.rem(band + halo - u * band + width, width), 1)
                for m in range(mains):
                    corr[u, slot_of(c, m)] = line[:, m * cols : (m + 1) * cols].astype(BF)
                piece = line[:, half_w : half_w + cols]
                e = c % pack
                if e:
                    piece = pltpu.roll(piece, e * edge, 1)
                    keep = jnp.logical_and(tile_lane >= e * edge, tile_lane < (e + 1) * edge)
                    edges[b] = jnp.where(keep, piece, edges[b])
                else:
                    edges[b] = jnp.where(tile_lane < edge, piece, 0.0)
                if e == pack - 1 or c == maps - 1:
                    corr[u, slot_of(c, mains - 1) + 1] = edges[b].astype(BF)
        for b in range(2):
            u = 2 * lot + b
            head = head_of(u, t, nh)

            @pl.when(head != h)
            def _():
                @pl.when(head > h)
                def _():
                    pl.semaphore_wait(ready.at[head], 1)
                remote(corr.at[u], got.at[h], gsend, grecv, head, t).start()
        return 0

    lax.fori_loop(0, lots, lot_step, 0)
    local = pltpu.make_async_copy(corr.at[here], got.at[h], lsem)
    local.start()

    def column(line):
        return jnp.broadcast_to(line, (8, feat)).T[:, 0:1]

    for copy in load_weights:
        copy.wait()
    for layer in range(layers):
        for half in range(2):
            for v in range(2):
                for i in range(3):
                    taken = [(i, j) if v == 0 else (j, i) for j in range(3)]
                    weights[layer, half, (3 * v + i) * feat : (3 * v + i + 1) * feat, :] = jnp.concatenate(
                        [cw_ref[layer, half, dy, dx].astype(F32) for dy, dx in taken], axis=1
                    ).astype(BF)
    proj_bias = column(pb_ref[...])
    place = lax.broadcasted_iota(jnp.int32, (nh * maps, nh * slots), 1)
    for m in range(mains + pack):
        chosen = jnp.where(place == tgt_ref[:, m : m + 1], 1.0, 0.0).astype(BF)
        pwide[m * feat : (m + 1) * feat, :] = jnp.dot(
            pw_ref[...], chosen, preferred_element_type=F32
        ).astype(BF)

    def neighbour(step):
        band_there = lax.rem(spot + nd + step, nd)
        tile = band_there // nh
        return head_of(lax.rem(band_there, nh), tile, nh), tile

    up_head, up_tile = neighbour(-1)
    down_head, down_tile = neighbour(1)
    last_group = rows // halo - 1
    def halo_copies(side):
        up = side == 0
        there = (jnp.where(up, up_head, down_head), jnp.where(up, up_tile, down_tile))
        rows_there = sm.at[0, pl.ds(jnp.where(up, halo + band, 0), halo)]
        edge_there = se.at[0, jnp.where(up, last_group, 0)]
        return (
            remote(um.at[side], rows_there, hsend.at[2 * side], hrecv.at[2 * side], *there),
            remote(ue.at[side], edge_there, hsend.at[2 * side + 1], hrecv.at[2 * side + 1], *there),
        )

    local.wait()
    rest = got.at[pl.ds(0, nh - 1)]
    pltpu.make_async_copy(rest, rest, grecv).wait()
    wide[...] = got[...].astype(F32).reshape(nh * slots * band, cols)
    lane_e = lax.broadcasted_iota(jnp.int32, (feat, cols), 1)
    for i in range(2):
        side = lax.rem(spot + i, 2)
        kept = sent = None
        for e in range(halo):
            r = side * halo + e
            x = wide[pl.ds(r, nh * slots, stride=band), :].astype(BF)
            value = jnp.dot(pwide[...], x, preferred_element_type=F32)
            if mains > 1:
                blocks = []
                for m in range(mains):
                    blocks.append(value[m * feat : (m + 1) * feat])
            else:
                blocks = [value[0:feat]]
            tail = value[mains * feat : (mains + 1) * feat]
            for f in range(1, pack):
                low = (mains + f) * feat
                tail = tail + jnp.where(
                    lane_e < edge, pltpu.roll(value[low : low + feat], cols - f * edge, 1), 0.0
                )
            line = jnp.concatenate(blocks + [tail], axis=1) + proj_bias
            sm[0, halo + r] = line[:, :half_w].astype(BF)
            shift = jnp.where(side == 0, band, half_w + cols - band)
            um[side, e] = pltpu.roll(line, shift, 1)[:, :half_w].astype(BF)
            pair = line[:, half_w - cols :]
            span = 2 * cols
            mine_at = cols - 2 * halo
            sent_at = jnp.where(side == 0, mine_at - band, mine_at + band)
            inside = jnp.logical_and(lane_e >= e * edge, lane_e < (e + 1) * edge)
            own_piece = pltpu.roll(pair, (span - mine_at + e * edge) % span, 1)[:, :cols]
            sent_piece = pltpu.roll(pair, lax.rem(span - sent_at + e * edge, span), 1)[:, :cols]
            kept = own_piece if kept is None else jnp.where(inside, own_piece, kept)
            sent = sent_piece if sent is None else jnp.where(inside, sent_piece, sent)
        se[0, 1 + side] = kept.astype(BF)
        ue[side] = sent.astype(BF)
        for copy in halo_copies(side):
            copy.start()

    first_row = spot * band - halo
    seam = lax.rem(band + halo - spot * band + width, width)
    before_seam = lax.rem(seam + width - 1, width)
    lane = lax.broadcasted_iota(jnp.int32, (feat, half_w), 1)
    lane_w = start + jnp.bitwise_and(lane_e, edge - 1)
    top_in = spot > 0
    bottom_in = spot < nd - 1

    def shifted(v, at, size):
        before = jnp.where(at == seam, 0.0, pltpu.roll(v, 1, 1))
        after = jnp.where(at == before_seam, 0.0, pltpu.roll(v, size - 1, 1))
        return before.astype(BF), v.astype(BF), after.astype(BF)

    def put(v, r, value, inside=None):
        if inside is not None:
            value = jnp.where(inside, value, 0.0)
        for i, x in enumerate(shifted(value, lane, half_w)):
            stack[v, r, i * feat : (i + 1) * feat] = x

    def put_edge(v, g, value):
        if g == 0:
            value = jnp.where(top_in, value, 0.0)
        if g == last_group:
            value = jnp.where(bottom_in, value, 0.0)
        for i, x in enumerate(shifted(value, lane_w, cols)):
            stack_e[v, g, i * feat : (i + 1) * feat] = x

    tall = 3 * feat

    def finish(v, tails):
        small = [
            pltpu.roll(line, (cols - e * edge) % cols, 1) for line in tails for e in range(pack)
        ]
        wide_main = jnp.concatenate(
            [final_rows[v], jnp.zeros((band, width - half_w), F32)], axis=1
        )
        wide_edge = jnp.concatenate(
            [jnp.concatenate(small, axis=0), jnp.zeros((band, width - cols), F32)], axis=1
        )
        at = lax.broadcasted_iota(jnp.int32, (band, width), 1)
        line = jnp.where(at < half_w - halo, wide_main, pltpu.roll(wide_edge, start, 1))
        line = pltpu.roll(line, lax.rem(spot * band - band - halo + width, width), 1)
        for p in range(nt):
            logits[v, p] = line[:, p * cols : (p + 1) * cols]

    readout = column(ow_ref[...])
    biases = [column(cb_ref[low // 2, low % 2 : low % 2 + 1, :]) for low in range(2 * layers)]
    last = 2 * layers - 1

    def weight(low, v):
        return weights[low // 2, low % 2, v * tall : (v + 1) * tall, :]

    def elu(x):
        return jnp.where(x > 0.0, x, jnp.exp(jnp.minimum(x, 0.0)) - 1.0)

    def product(low, source, store, these):
        for n in range(0, len(these), 2):
            two = these[n : n + 2]
            for v in range(1 if low == 0 else 2):
                x = jnp.concatenate([source[v, r] for r in two], axis=1)
                w = weights[0, 0] if low == 0 else weight(low, v)
                block = jnp.dot(w, x, preferred_element_type=F32)
                size = block.shape[1] // len(two)
                for i, r in enumerate(two):
                    got_r = block[:, i * size : (i + 1) * size]
                    if low == 0:
                        store(0, r, got_r[:tall])
                        store(1, r, got_r[tall:])
                    else:
                        store(v, r, got_r)

    def multiply(low, these, inside=None):
        if low == 0:
            for r in these:
                put(0, r, sm[0, r].astype(F32), inside and inside(r))

        def store(v, r, x):
            taps[low % 2, v, r] = x

        product(low, stack, store, these)

    def gather(low, s, inside=None):
        for v in range(2):
            part = taps.at[low % 2, v]
            conv = part[s - 1, 0:feat] + part[s, feat : 2 * feat] + part[s + 1, 2 * feat :] + biases[low]
            if low % 2 == 0:
                put(v, s, elu(conv), inside)
                continue
            value = (sm[0 if low == 1 else 1 + v, s].astype(F32) + conv).astype(BF)
            if low < last:
                sm[1 + v, s] = value
                put(v, s, value.astype(F32), inside)
            else:
                final_rows[v, pl.ds(s - halo, 1), :] = jnp.sum(
                    value.astype(F32) * readout, axis=0, keepdims=True
                )

    def multiply_edges(low):
        these = list(range(last_group + 1))
        if low == 0:
            for g in these:
                put_edge(0, g, se[0, g].astype(F32))

        def store(v, g, x):
            taps_e[v, g] = x

        product(low, stack_e, store, these)

    def gather_edges(low):
        for v in range(2):
            tails = []
            for g in range(1, last_group) if low == last else range(last_group + 1):
                over, under = max(g - 1, 0), min(g + 1, last_group)
                upper = jnp.where(lane_e >= cols - edge, taps_e[v, over, 0:feat], taps_e[v, g, 0:feat])
                lower = jnp.where(lane_e < edge, taps_e[v, under, 2 * feat :], taps_e[v, g, 2 * feat :])
                conv = (
                    pltpu.roll(upper, edge, 1) + taps_e[v, g, feat : 2 * feat]
                    + pltpu.roll(lower, cols - edge, 1) + biases[low]
                )
                if low % 2 == 0:
                    put_edge(v, g, elu(conv))
                    continue
                value = (se[0 if low == 1 else 1 + v, g].astype(F32) + conv).astype(BF)
                if low < last:
                    se[1 + v, g] = value
                    put_edge(v, g, value.astype(F32))
                else:
                    tails.append(jnp.sum(value.astype(F32) * readout, axis=0, keepdims=True))
            if low == last:
                finish(v, tails)

    for low in range(2 * layers):
        early = range(halo + low, halo + band - low)
        multiply(low, list(early))
        for s in early[1:-1]:
            gather(low, s)

    def await_halo(below):
        fringe = sm.at[0, pl.ds(halo + band if below else 0, halo)]
        corner = se.at[0, last_group if below else 0]
        came = 0 if below else 2
        pltpu.make_async_copy(fringe, fringe, hrecv.at[came]).wait()
        pltpu.make_async_copy(corner, corner, hrecv.at[came + 1]).wait()

    def inside(r):
        if r < halo:
            return top_in
        return bottom_in if r >= halo + band else None

    def late():
        for low in range(2 * layers):
            these = [r for n in range(low, halo + low) for r in (n, rows - 1 - n)]
            multiply(low, these, inside)
            multiply_edges(low)
            for n in range(low + 1, halo + low + 1):
                for s in (n, rows - 1 - n):
                    gather(low, s, inside(s))
            gather_edges(low)

    for below in (False, True):
        await_halo(below)
    late()

    owner, slot = spot // nt, lax.rem(spot, nt)

    def deliver(k):
        p = lax.rem(t + k, nt)
        return remote(
            logits.at[0, p], rows_w.at[slot], osend.at[k], orecv.at[slot], owner, p,
        )

    def turn(head):
        return logits.at[1, head * nt * band // cols]

    def wanted(col, head):
        far_off = lax.rem(col - head * nt + nd, nd)
        return jnp.logical_or(far_off > nd // 2, lax.rem(far_off - (nt - 1) + nd, nd) > nd // 2)

    def send_turned(i, _):
        head = lax.rem(h + i, nh)

        @pl.when(wanted(spot, head))
        def _():
            remote(
                turn(head), rows_t.at[here], tsend.at[head], trecv.at[here], head, t
            ).start()
        return 0

    for k in range(1, nt):
        deliver(k).start()
    lax.fori_loop(1, nh, send_turned, 0)

    @pl.when(owner == h)
    def _():
        pltpu.make_async_copy(logits.at[0, t], rows_w.at[slot], orecv.at[slot]).start()

    @pl.when(owner != h)
    def _():
        deliver(0).start()

    rows_t[here] = logits[1, h * nt * band // cols]
    one = rows_t.at[0]

    def await_piece(i, _):
        @pl.when(jnp.logical_and(i != here, wanted(t * nh + i, h)))
        def _():
            pltpu.make_async_copy(one, one, trecv.at[i]).wait()
        return 0

    lax.fori_loop(0, nh, await_piece, 0)
    turned[...] = rows_t[...].reshape(nh * band, cols).T
    for k in range(nt):
        pltpu.make_async_copy(logits.at[0, k], rows_w.at[k], orecv.at[k]).wait()
    block = turned[pl.ds(pl.multiple_of(lax.rem(h * nt * band, cols), nt * band), nt * band), :]
    shape = (nt, band, cols)
    row_band = h * nt + lax.broadcasted_iota(jnp.int32, shape, 0)
    col_band = t * nh + jnp.right_shift(lax.broadcasted_iota(jnp.int32, shape, 2), band.bit_length() - 1)
    away = col_band - row_band
    away = jnp.where(away < 0, away + nd, away)
    out_ref[...] = jnp.where(away <= nd // 2, rows_w[...], block.reshape(shape))

    @pl.when(owner != h)
    def _():
        deliver(0).wait_send()

    for k in range(1, nt):
        deliver(k).wait_send()
        parts_copy(k).wait_send()
        for j in range(lots):
            mirror_copy(k, j, True).wait_send()
    for side in range(2):
        for copy in halo_copies(side):
            copy.wait_send()
    pltpu.make_async_copy(rest, rest, gsend).wait()

    def sent(i, _):
        head = lax.rem(h + i, nh)

        @pl.when(wanted(spot, head))
        def _():
            pltpu.make_async_copy(one, one, tsend.at[head]).wait()
        return 0

    lax.fori_loop(1, nh, sent, 0)


def in_hbm(x):
    return pltpu.with_memory_space_constraint(x, pltpu.HBM)


def on_device(attention, proj_weight, proj_bias, conv_weight, conv_bias, out_weight):
    nh, nt = lax.axis_size("head"), lax.axis_size("tile")
    nd = nh * nt
    maps, width, cols = attention.shape
    layers, two, feat = conv_weight.shape[:3]
    band = width // nd
    far = max(nt - 1, 1)
    halo = 2 * layers
    rows = band + 2 * halo
    half_w = width // 2
    mains = half_w // cols
    pack = cols // (3 * band + 2 * halo)
    assert pack == halo and band == 2 * halo and nh * band == cols
    groups = [range(g, min(g + pack, maps)) for g in range(0, maps, pack)]
    slots = maps * mains + len(groups)
    count = rows // halo
    ordered = jnp.transpose(conv_weight, (0, 1, 4, 5, 2, 3))
    target = np.full((nh * maps, mains + pack), -1, np.int32)
    for src in range(nh):
        for c in range(maps):
            g = c // pack
            for m in range(mains):
                target[src * maps + c, m] = src * slots + c * mains + m + g
            target[src * maps + c, mains + c % pack] = src * slots + groups[g].stop * mains + g
    dma = pltpu.SemaphoreType.DMA
    out = pl.pallas_call(
        functools.partial(kernel, nh, nt),
        out_shape=jax.ShapeDtypeStruct((nt, band, cols), F32),
        in_specs=[pl.BlockSpec(memory_space=pltpu.HBM)] * 7,
        out_specs=pl.BlockSpec(memory_space=VM),
        scratch_shapes=[
            VM((maps, width, cols), BF),
            VM(proj_weight.shape, BF),
            VM((1, feat), F32),
            VM(ordered.shape, BF),
            VM(conv_bias.shape, F32),
            VM((1, feat), F32),
            VM(target.shape, jnp.int32),
            VM((nt, maps, cols, cols), BF),
            VM((maps, cols, cols), F32),
            VM((far, maps, cols, cols), F32),
            VM((cols, maps), F32),
            VM((maps, width), F32),
            VM((maps, width), F32),
            VM((far, maps, width), F32),
            VM((nh, slots, band, cols), BF),
            VM((nh, slots, band, cols), BF),
            VM((nh * slots * band, cols), F32),
            VM(((mains + pack) * feat, nh * slots), BF),
            VM((layers, two, 6 * feat, 3 * feat), BF),
            VM((3, rows, feat, half_w), BF),
            VM((3, count, feat, cols), BF),
            VM((2, halo, feat, half_w), BF),
            VM((2, feat, cols), BF),
            VM((2, rows, 3 * feat, half_w), BF),
            VM((2, count, 3 * feat, cols), BF),
            VM((2, 2, rows, 3 * feat, half_w), F32),
            VM((2, count, 3 * feat, cols), F32),
            VM((2, band, half_w), F32),
            VM((2, nt, band, cols), F32),
            VM((nt, band, cols), F32),
            VM((nh, band, cols), F32),
            VM((cols, cols), F32),
            dma,
            dma((6,)),
            dma((far, nh // 2)),
            dma((far, nh // 2)),
            dma((far,)),
            dma((far,)),
            dma,
            dma,
            dma,
            dma((4,)),
            dma((4,)),
            dma((nt,)),
            dma((nt,)),
            dma((nh,)),
            dma((nh,)),
            pltpu.SemaphoreType.REGULAR((nh,)),
        ],
        compiler_params=pltpu.CompilerParams(
            collective_id=0, has_side_effects=True, vmem_limit_bytes=53 * 1024 * 1024
        ),
        name="head",
    )(*map(in_hbm, (
        attention, proj_weight, proj_bias[None], ordered, conv_bias, out_weight[None], jnp.asarray(target),
    )))
    return out.reshape(nt * band, cols)


def solution(mesh):
    return jax.shard_map(
        on_device,
        mesh=mesh,
        in_specs=(P(("grp", "head"), None, "tile"), P(), P(), P(), P(), P()),
        out_specs=P(("grp", "head"), "tile"),
        check_vma=False,
    )
```

```python
import functools
import jax
import jax.numpy as jnp
import numpy as np
from jax import lax
from jax.experimental import pallas as pl
from jax.experimental.pallas import tpu as pltpu
from jax.sharding import PartitionSpec as P

VM = pltpu.VMEM
BF = jnp.bfloat16
F32 = jnp.float32
MESH = pl.DeviceIdType.MESH


def remote(src, dst, send, recv, head, tile):
    return pltpu.make_async_remote_copy(
        src_ref=src,
        dst_ref=dst,
        send_sem=send,
        recv_sem=recv,
        device_id={"head": head, "tile": tile},
        device_id_type=MESH,
    )


def fold(head):
    pair, core = head // 2, lax.rem(head, 2)
    row, col = pair // 2, lax.rem(pair, 2)
    col = jnp.where(lax.rem(row, 2) == 0, col, 1 - col)
    return (row * 2 + col) * 2 + core


def spot_of(head, tile, nh):
    place = fold(head)
    return jnp.where(lax.rem(tile, 2) == 0, place, nh - 1 - place)


def head_of(spot, tile, nh):
    return fold(jnp.where(lax.rem(tile, 2) == 0, spot, nh - 1 - spot))


def kernel(
    nh, nt, a_hbm, pw_hbm, pb_hbm, cw_hbm, cb_hbm, ow_hbm, tgt_hbm, out_ref,
    a_ref, pw_ref, pb_ref, cw_ref, cb_ref, ow_ref, tgt_ref, mirror, both, upright, scaled, own, total, parts, corr, got, wide, pwide, weights,
    sm, se, um, ue, stack, stack_e, taps, taps_e, final_rows, logits, rows_w, rows_t, turned,
    asem, wsem, msend, mrecv, psend, precv, gsend, grecv, lsem,
    hsend, hrecv, osend, orecv, tsend, trecv, ready,
):
    maps, width, cols = a_ref.shape
    slots, band = got.shape[1:3]
    nd = nh * nt
    half_w = width // 2
    mains = half_w // cols
    feat = pw_ref.shape[0]
    layers = cw_ref.shape[0]
    halo = 2 * layers
    rows = band + 2 * halo
    edge = 3 * band + 2 * halo
    pack = cols // edge
    start = half_w - 2 * halo
    h = lax.axis_index("head")
    t = lax.axis_index("tile")
    here = spot_of(h, t, nh)
    spot = t * nh + here

    def slot_of(c, m=0):
        return c * mains + m + c // pack

    load = pltpu.make_async_copy(a_hbm, a_ref, asem)
    load.start()
    barrier = pltpu.get_barrier_semaphore()

    def greet(head, tile):
        pl.semaphore_signal(
            barrier, inc=1, device_id={"head": head, "tile": tile}, device_id_type=MESH
        )

    for k in range(1, nt):
        greet(h, lax.rem(t + k, nt))

    def greet_later(i, _):
        greet(i, t)
        return 0

    lax.fori_loop(h + 1, nh, greet_later, 0)
    load_weights = [
        pltpu.make_async_copy(src, dst, wsem.at[i])
        for i, (src, dst) in enumerate((
            (cw_hbm, cw_ref), (pw_hbm, pw_ref), (pb_hbm, pb_ref), (cb_hbm, cb_ref), (ow_hbm, ow_ref),
            (tgt_hbm, tgt_ref),
        ))
    ]
    for copy in load_weights:
        copy.start()
    pl.semaphore_wait(barrier, nt - 1 + h)

    def tell_earlier(i, _):
        pl.semaphore_signal(
            ready.at[h], inc=1, device_id={"head": i, "tile": t}, device_id_type=MESH
        )
        return 0

    lots = nh // 2
    step_rows = 2 * band

    def lot_of(j, tile):
        other = (h < nh // 2) == (lax.rem(tile, 2) == 0)
        return lax.rem(j + jnp.where(other, lots // 2, 0), lots)

    def mirror_copy(k, j, to):
        p = lax.rem(t + k, nt)
        low = pl.multiple_of(lot_of(j, p if to else t) * step_rows, step_rows)
        return remote(
            a_hbm.at[:, pl.ds(pl.multiple_of(p * cols + low, step_rows), step_rows), :],
            mirror.at[t, :, pl.ds(low, step_rows)],
            msend.at[k - 1, j], mrecv.at[k - 1, j], h, p,
        )

    def parts_copy(k):
        p = lax.rem(t + k, nt)
        return remote(own, parts.at[k - 1], psend.at[k - 1], precv.at[k - 1], h, p)

    for k in range(1, nt):
        mirror_copy(k, 0, True).start()
    lax.fori_loop(0, h, tell_earlier, 0)

    load.wait()
    mine = pl.ds(pl.multiple_of(t * cols, cols), cols)
    ones_t = jnp.ones((8, cols), BF)
    ones_w = jnp.ones((8, width), BF)
    for c in range(maps):
        a = a_ref[c]
        line = lax.dot_general(ones_t, a, (((1,), (1,)), ((), ())), preferred_element_type=F32)
        own[c : c + 1, :] = line[0:1]
        columns = jnp.dot(ones_w, a, preferred_element_type=F32)
        own[c : c + 1, mine] = own[c : c + 1, mine] + columns[0:1]
    for k in range(1, nt):
        parts_copy(k).start()
    for k in range(1, nt):
        for j in range(1, lots):
            mirror_copy(k, j, True).start()
    for c in range(maps):
        a = a_ref[c, mine, :].astype(F32)
        both[c] = a + a.T
        for k in range(1, nt):
            at = pl.ds(pl.multiple_of(lax.rem(t + k, nt) * cols, cols), cols)
            upright[k - 1, c] = a_ref[c, at, :].astype(F32).T
    for k in range(1, nt):
        parts_copy(k).wait_recv()
    sums = own[...]
    for k in range(1, nt):
        sums = sums + parts[k - 1]
    total[...] = sums
    grand = jnp.sum(sums, axis=1, keepdims=True)
    scaled[...] = (total[:, mine] / grand).T

    tile_lane = lax.broadcasted_iota(jnp.int32, (band, cols), 1)

    def lot_step(j, _):
        lot = lot_of(j, t)
        these = pl.ds(pl.multiple_of(lot * step_rows, step_rows), step_rows)
        for k in range(1, nt):
            mirror_copy(k, j, False).wait_recv()
        factor = scaled[these, :]
        edges = [None, None]
        for c in range(maps):
            pieces = []
            for k in range(nt):
                p = lax.rem(t + k, nt)
                at = pl.ds(pl.multiple_of(p * cols, cols), cols)
                if k:
                    sym = mirror[p, c, these, :].astype(F32) + upright[k - 1, c, these, :]
                else:
                    sym = both[c, these, :]
                pieces.append(sym - factor[:, c : c + 1] * total[c : c + 1, at])
            value = jnp.concatenate(pieces, axis=1)
            for b in range(2):
                u = 2 * lot + b
                line = value[b * band : (b + 1) * band]
                line = pltpu.roll(line, lax.rem(band + halo - u * band + width, width), 1)
                for m in range(mains):
                    corr[u, slot_of(c, m)] = line[:, m * cols : (m + 1) * cols].astype(BF)
                piece = line[:, half_w : half_w + cols]
                e = c % pack
                if e:
                    piece = pltpu.roll(piece, e * edge, 1)
                    keep = jnp.logical_and(tile_lane >= e * edge, tile_lane < (e + 1) * edge)
                    edges[b] = jnp.where(keep, piece, edges[b])
                else:
                    edges[b] = jnp.where(tile_lane < edge, piece, 0.0)
                if e == pack - 1 or c == maps - 1:
                    corr[u, slot_of(c, mains - 1) + 1] = edges[b].astype(BF)
        for b in range(2):
            u = 2 * lot + b
            head = head_of(u, t, nh)

            @pl.when(head != h)
            def _():
                @pl.when(head > h)
                def _():
                    pl.semaphore_wait(ready.at[head], 1)
                remote(corr.at[u], got.at[h], gsend, grecv, head, t).start()
        return 0

    lax.fori_loop(0, lots, lot_step, 0)
    local = pltpu.make_async_copy(corr.at[here], got.at[h], lsem)
    local.start()

    def column(line):
        return jnp.broadcast_to(line, (8, feat)).T[:, 0:1]

    for copy in load_weights:
        copy.wait()
    for layer in range(layers):
        for half in range(2):
            for v in range(2):
                for i in range(3):
                    taken = [(i, j) if v == 0 else (j, i) for j in range(3)]
                    weights[layer, half, (3 * v + i) * feat : (3 * v + i + 1) * feat, :] = jnp.concatenate(
                        [cw_ref[layer, half, dy, dx].astype(F32) for dy, dx in taken], axis=1
                    ).astype(BF)
    proj_bias = column(pb_ref[...])
    place = lax.broadcasted_iota(jnp.int32, (nh * maps, nh * slots), 1)
    for m in range(mains + pack):
        chosen = jnp.where(place == tgt_ref[:, m : m + 1], 1.0, 0.0).astype(BF)
        pwide[m * feat : (m + 1) * feat, :] = jnp.dot(
            pw_ref[...], chosen, preferred_element_type=F32
        ).astype(BF)

    def neighbour(step):
        band_there = lax.rem(spot + nd + step, nd)
        tile = band_there // nh
        return head_of(lax.rem(band_there, nh), tile, nh), tile

    up_head, up_tile = neighbour(-1)
    down_head, down_tile = neighbour(1)
    last_group = rows // halo - 1
    def halo_copies(side):
        up = side == 0
        there = (jnp.where(up, up_head, down_head), jnp.where(up, up_tile, down_tile))
        lead = halo // 2
        low = jnp.where(up, halo + band, 0)
        edge_there = se.at[0, jnp.where(up, last_group, 0)]
        pairs = (
            (um.at[side, pl.ds(0, lead)], sm.at[0, pl.ds(low, lead)]),
            (um.at[side, pl.ds(lead, halo - lead)], sm.at[0, pl.ds(low + lead, halo - lead)]),
            (ue.at[side], edge_there),
        )
        return [
            remote(src, dst, hsend.at[3 * side + i], hrecv.at[3 * side + i], *there)
            for i, (src, dst) in enumerate(pairs)
        ]

    local.wait()
    rest = got.at[pl.ds(0, nh - 1)]
    pltpu.make_async_copy(rest, rest, grecv).wait()
    wide[...] = got[...].astype(F32).reshape(nh * slots * band, cols)
    lane_e = lax.broadcasted_iota(jnp.int32, (feat, cols), 1)
    for i in range(2):
        side = lax.rem(spot + i, 2)
        kept = sent = None
        for e in range(halo):
            r = side * halo + e
            x = wide[pl.ds(r, nh * slots, stride=band), :].astype(BF)
            value = jnp.dot(pwide[...], x, preferred_element_type=F32)
            if mains > 1:
                blocks = []
                for m in range(mains):
                    blocks.append(value[m * feat : (m + 1) * feat])
            else:
                blocks = [value[0:feat]]
            tail = value[mains * feat : (mains + 1) * feat]
            for f in range(1, pack):
                low = (mains + f) * feat
                tail = tail + jnp.where(
                    lane_e < edge, pltpu.roll(value[low : low + feat], cols - f * edge, 1), 0.0
                )
            line = jnp.concatenate(blocks + [tail], axis=1) + proj_bias
            sm[0, halo + r] = line[:, :half_w].astype(BF)
            shift = jnp.where(side == 0, band, half_w + cols - band)
            um[side, e] = pltpu.roll(line, shift, 1)[:, :half_w].astype(BF)
            if e == halo // 2 - 1:
                halo_copies(side)[0].start()
            pair = line[:, half_w - cols :]
            span = 2 * cols
            mine_at = cols - 2 * halo
            sent_at = jnp.where(side == 0, mine_at - band, mine_at + band)
            inside = jnp.logical_and(lane_e >= e * edge, lane_e < (e + 1) * edge)
            own_piece = pltpu.roll(pair, (span - mine_at + e * edge) % span, 1)[:, :cols]
            sent_piece = pltpu.roll(pair, lax.rem(span - sent_at + e * edge, span), 1)[:, :cols]
            kept = own_piece if kept is None else jnp.where(inside, own_piece, kept)
            sent = sent_piece if sent is None else jnp.where(inside, sent_piece, sent)
        se[0, 1 + side] = kept.astype(BF)
        ue[side] = sent.astype(BF)
        for copy in halo_copies(side)[1:]:
            copy.start()

    first_row = spot * band - halo
    seam = lax.rem(band + halo - spot * band + width, width)
    before_seam = lax.rem(seam + width - 1, width)
    lane = lax.broadcasted_iota(jnp.int32, (feat, half_w), 1)
    lane_w = start + jnp.bitwise_and(lane_e, edge - 1)
    top_in = spot > 0
    bottom_in = spot < nd - 1

    def shifted(v, at, size):
        before = jnp.where(at == seam, 0.0, pltpu.roll(v, 1, 1))
        after = jnp.where(at == before_seam, 0.0, pltpu.roll(v, size - 1, 1))
        return before.astype(BF), v.astype(BF), after.astype(BF)

    def put(v, r, value, inside=None):
        if inside is not None:
            value = jnp.where(inside, value, 0.0)
        for i, x in enumerate(shifted(value, lane, half_w)):
            stack[v, r, i * feat : (i + 1) * feat] = x

    def put_edge(v, g, value):
        if g == 0:
            value = jnp.where(top_in, value, 0.0)
        if g == last_group:
            value = jnp.where(bottom_in, value, 0.0)
        for i, x in enumerate(shifted(value, lane_w, cols)):
            stack_e[v, g, i * feat : (i + 1) * feat] = x

    tall = 3 * feat

    def finish(v, tails):
        small = [
            pltpu.roll(line, (cols - e * edge) % cols, 1) for line in tails for e in range(pack)
        ]
        wide_main = jnp.concatenate(
            [final_rows[v], jnp.zeros((band, width - half_w), F32)], axis=1
        )
        wide_edge = jnp.concatenate(
            [jnp.concatenate(small, axis=0), jnp.zeros((band, width - cols), F32)], axis=1
        )
        at = lax.broadcasted_iota(jnp.int32, (band, width), 1)
        line = jnp.where(at < half_w - halo, wide_main, pltpu.roll(wide_edge, start, 1))
        line = pltpu.roll(line, lax.rem(spot * band - band - halo + width, width), 1)
        for p in range(nt):
            logits[v, p] = line[:, p * cols : (p + 1) * cols]

    readout = column(ow_ref[...])
    biases = [column(cb_ref[low // 2, low % 2 : low % 2 + 1, :]) for low in range(2 * layers)]
    last = 2 * layers - 1

    def weight(low, v):
        return weights[low // 2, low % 2, v * tall : (v + 1) * tall, :]

    def elu(x):
        return jnp.where(x > 0.0, x, jnp.exp(jnp.minimum(x, 0.0)) - 1.0)

    def product(low, source, store, these):
        for n in range(0, len(these), 2):
            two = these[n : n + 2]
            for v in range(1 if low == 0 else 2):
                x = jnp.concatenate([source[v, r] for r in two], axis=1)
                w = weights[0, 0] if low == 0 else weight(low, v)
                block = jnp.dot(w, x, preferred_element_type=F32)
                size = block.shape[1] // len(two)
                for i, r in enumerate(two):
                    got_r = block[:, i * size : (i + 1) * size]
                    if low == 0:
                        store(0, r, got_r[:tall])
                        store(1, r, got_r[tall:])
                    else:
                        store(v, r, got_r)

    def multiply(low, these, inside=None):
        if low == 0:
            for r in these:
                put(0, r, sm[0, r].astype(F32), inside and inside(r))

        def store(v, r, x):
            taps[low % 2, v, r] = x

        product(low, stack, store, these)

    def gather(low, s, inside=None):
        for v in range(2):
            part = taps.at[low % 2, v]
            conv = part[s - 1, 0:feat] + part[s, feat : 2 * feat] + part[s + 1, 2 * feat :] + biases[low]
            if low % 2 == 0:
                put(v, s, elu(conv), inside)
                continue
            value = (sm[0 if low == 1 else 1 + v, s].astype(F32) + conv).astype(BF)
            if low < last:
                sm[1 + v, s] = value
                put(v, s, value.astype(F32), inside)
            else:
                final_rows[v, pl.ds(s - halo, 1), :] = jnp.sum(
                    value.astype(F32) * readout, axis=0, keepdims=True
                )

    def multiply_edges(low):
        these = list(range(last_group + 1))
        if low == 0:
            for g in these:
                put_edge(0, g, se[0, g].astype(F32))

        def store(v, g, x):
            taps_e[v, g] = x

        product(low, stack_e, store, these)

    def gather_edges(low):
        for v in range(2):
            tails = []
            for g in range(1, last_group) if low == last else range(last_group + 1):
                over, under = max(g - 1, 0), min(g + 1, last_group)
                upper = jnp.where(lane_e >= cols - edge, taps_e[v, over, 0:feat], taps_e[v, g, 0:feat])
                lower = jnp.where(lane_e < edge, taps_e[v, under, 2 * feat :], taps_e[v, g, 2 * feat :])
                conv = (
                    pltpu.roll(upper, edge, 1) + taps_e[v, g, feat : 2 * feat]
                    + pltpu.roll(lower, cols - edge, 1) + biases[low]
                )
                if low % 2 == 0:
                    put_edge(v, g, elu(conv))
                    continue
                value = (se[0 if low == 1 else 1 + v, g].astype(F32) + conv).astype(BF)
                if low < last:
                    se[1 + v, g] = value
                    put_edge(v, g, value.astype(F32))
                else:
                    tails.append(jnp.sum(value.astype(F32) * readout, axis=0, keepdims=True))
            if low == last:
                finish(v, tails)

    for low in range(2 * layers):
        early = range(halo + low, halo + band - low)
        multiply(low, list(early))
        for s in early[1:-1]:
            gather(low, s)

    def await_halo(below):
        low = halo + band if below else 0
        came = 0 if below else 3
        lead = halo // 2
        for i, landed in enumerate((
            sm.at[0, pl.ds(low, lead)], sm.at[0, pl.ds(low + lead, halo - lead)],
            se.at[0, last_group if below else 0],
        )):
            pltpu.make_async_copy(landed, landed, hrecv.at[came + i]).wait()

    def inside(r):
        if r < halo:
            return top_in
        return bottom_in if r >= halo + band else None

    def late():
        for low in range(2 * layers):
            these = [r for n in range(low, halo + low) for r in (n, rows - 1 - n)]
            multiply(low, these, inside)
            multiply_edges(low)
            for n in range(low + 1, halo + low + 1):
                for s in (n, rows - 1 - n):
                    gather(low, s, inside(s))
            gather_edges(low)

    for below in (False, True):
        await_halo(below)
    late()

    owner, slot = spot // nt, lax.rem(spot, nt)

    def deliver(k):
        p = lax.rem(t + k, nt)
        return remote(
            logits.at[0, p], rows_w.at[slot], osend.at[k], orecv.at[slot], owner, p,
        )

    def turn(head):
        return logits.at[1, head * nt * band // cols]

    def wanted(col, head):
        far_off = lax.rem(col - head * nt + nd, nd)
        return jnp.logical_or(far_off > nd // 2, lax.rem(far_off - (nt - 1) + nd, nd) > nd // 2)

    def send_turned(i, _):
        head = lax.rem(h + i, nh)

        @pl.when(wanted(spot, head))
        def _():
            remote(
                turn(head), rows_t.at[here], tsend.at[head], trecv.at[here], head, t
            ).start()
        return 0

    for k in range(1, nt):
        deliver(k).start()
    lax.fori_loop(1, nh, send_turned, 0)

    @pl.when(owner == h)
    def _():
        pltpu.make_async_copy(logits.at[0, t], rows_w.at[slot], orecv.at[slot]).start()

    @pl.when(owner != h)
    def _():
        deliver(0).start()

    rows_t[here] = logits[1, h * nt * band // cols]
    one = rows_t.at[0]

    def await_piece(i, _):
        @pl.when(jnp.logical_and(i != here, wanted(t * nh + i, h)))
        def _():
            pltpu.make_async_copy(one, one, trecv.at[i]).wait()
        return 0

    lax.fori_loop(0, nh, await_piece, 0)
    turned[...] = rows_t[...].reshape(nh * band, cols).T
    for k in range(nt):
        pltpu.make_async_copy(logits.at[0, k], rows_w.at[k], orecv.at[k]).wait()
    block = turned[pl.ds(pl.multiple_of(lax.rem(h * nt * band, cols), nt * band), nt * band), :]
    shape = (nt, band, cols)
    row_band = h * nt + lax.broadcasted_iota(jnp.int32, shape, 0)
    col_band = t * nh + jnp.right_shift(lax.broadcasted_iota(jnp.int32, shape, 2), band.bit_length() - 1)
    away = col_band - row_band
    away = jnp.where(away < 0, away + nd, away)
    out_ref[...] = jnp.where(away <= nd // 2, rows_w[...], block.reshape(shape))

    @pl.when(owner != h)
    def _():
        deliver(0).wait_send()

    for k in range(1, nt):
        deliver(k).wait_send()
        parts_copy(k).wait_send()
        for j in range(lots):
            mirror_copy(k, j, True).wait_send()
    for side in range(2):
        for copy in halo_copies(side):
            copy.wait_send()
    pltpu.make_async_copy(rest, rest, gsend).wait()

    def sent(i, _):
        head = lax.rem(h + i, nh)

        @pl.when(wanted(spot, head))
        def _():
            pltpu.make_async_copy(one, one, tsend.at[head]).wait()
        return 0

    lax.fori_loop(1, nh, sent, 0)


def in_hbm(x):
    return pltpu.with_memory_space_constraint(x, pltpu.HBM)


def on_device(attention, proj_weight, proj_bias, conv_weight, conv_bias, out_weight):
    nh, nt = lax.axis_size("head"), lax.axis_size("tile")
    nd = nh * nt
    maps, width, cols = attention.shape
    layers, two, feat = conv_weight.shape[:3]
    band = width // nd
    far = max(nt - 1, 1)
    halo = 2 * layers
    rows = band + 2 * halo
    half_w = width // 2
    mains = half_w // cols
    pack = cols // (3 * band + 2 * halo)
    assert pack == halo and band == 2 * halo and nh * band == cols
    groups = [range(g, min(g + pack, maps)) for g in range(0, maps, pack)]
    slots = maps * mains + len(groups)
    count = rows // halo
    ordered = jnp.transpose(conv_weight, (0, 1, 4, 5, 2, 3))
    target = np.full((nh * maps, mains + pack), -1, np.int32)
    for src in range(nh):
        for c in range(maps):
            g = c // pack
            for m in range(mains):
                target[src * maps + c, m] = src * slots + c * mains + m + g
            target[src * maps + c, mains + c % pack] = src * slots + groups[g].stop * mains + g
    dma = pltpu.SemaphoreType.DMA
    out = pl.pallas_call(
        functools.partial(kernel, nh, nt),
        out_shape=jax.ShapeDtypeStruct((nt, band, cols), F32),
        in_specs=[pl.BlockSpec(memory_space=pltpu.HBM)] * 7,
        out_specs=pl.BlockSpec(memory_space=VM),
        scratch_shapes=[
            VM((maps, width, cols), BF),
            VM(proj_weight.shape, BF),
            VM((1, feat), F32),
            VM(ordered.shape, BF),
            VM(conv_bias.shape, F32),
            VM((1, feat), F32),
            VM(target.shape, jnp.int32),
            VM((nt, maps, cols, cols), BF),
            VM((maps, cols, cols), F32),
            VM((far, maps, cols, cols), F32),
            VM((cols, maps), F32),
            VM((maps, width), F32),
            VM((maps, width), F32),
            VM((far, maps, width), F32),
            VM((nh, slots, band, cols), BF),
            VM((nh, slots, band, cols), BF),
            VM((nh * slots * band, cols), F32),
            VM(((mains + pack) * feat, nh * slots), BF),
            VM((layers, two, 6 * feat, 3 * feat), BF),
            VM((3, rows, feat, half_w), BF),
            VM((3, count, feat, cols), BF),
            VM((2, halo, feat, half_w), BF),
            VM((2, feat, cols), BF),
            VM((2, rows, 3 * feat, half_w), BF),
            VM((2, count, 3 * feat, cols), BF),
            VM((2, 2, rows, 3 * feat, half_w), F32),
            VM((2, count, 3 * feat, cols), F32),
            VM((2, band, half_w), F32),
            VM((2, nt, band, cols), F32),
            VM((nt, band, cols), F32),
            VM((nh, band, cols), F32),
            VM((cols, cols), F32),
            dma,
            dma((6,)),
            dma((far, nh // 2)),
            dma((far, nh // 2)),
            dma((far,)),
            dma((far,)),
            dma,
            dma,
            dma,
            dma((6,)),
            dma((6,)),
            dma((nt,)),
            dma((nt,)),
            dma((nh,)),
            dma((nh,)),
            pltpu.SemaphoreType.REGULAR((nh,)),
        ],
        compiler_params=pltpu.CompilerParams(
            collective_id=0, has_side_effects=True, vmem_limit_bytes=53 * 1024 * 1024
        ),
        name="head",
    )(*map(in_hbm, (
        attention, proj_weight, proj_bias[None], ordered, conv_bias, out_weight[None], jnp.asarray(target),
    )))
    return out.reshape(nt * band, cols)


def solution(mesh):
    return jax.shard_map(
        on_device,
        mesh=mesh,
        in_specs=(P(("grp", "head"), None, "tile"), P(), P(), P(), P(), P()),
        out_specs=P(("grp", "head"), "tile"),
        check_vma=False,
    )
```
